32 devices in a mesh: seq: 8 (over z, x), chan: 4 (over y, core).
Axes of the slice: x: 2, y: 2, z: 4, core: 2. Of those that a mesh axis runs over, the one named last changes fastest.
Arguments:
- stream_in: bfloat16 [1024, 8192], P('seq', 'chan'), may hold values from -6 to 6
- features: bfloat16 [3, 1024, 8192], P(None, 'seq', 'chan'), may hold values from -6 to 6
- conv_taps: float32 [3, 3, 8192], P(None, None, 'chan'), may hold values from -3.5 to 3.5
- decay: float32 [8192, 8], P('chan'), may hold values from 0 to 1, as said below
- residues: float32 [8192, 8], P('chan'), may hold values from -1 to 1
- state_in: float32 [8192, 8], P('chan'), may hold values from -800 to 800
- out_weight: bfloat16 [8192, 8192], P('seq', 'chan'), may hold values from -0.0625 to 0.0625
Outputs:
- block_out: bfloat16 [1024, 8192], P('seq', 'chan')
The draws below stay inside these ranges and needn't reach their ends.
Inputs may be any that keep to these rules, and one draw needn't show every extreme that they name: `decay`: every rate is positive.
All inputs are finite; a program needn't handle non-finite values.
Results may differ from the reference program's by a relative error of at most 0.0046.
Values may be sent and summed in bfloat16 or wider, within the bound.
No kernel may reach another device: no remote copies, remote signals or barrier semaphores. Data moves between devices by JAX's collectives and lax.ppermute only.
A program may use at most 128 MiB of HBM per device.

```python
import math
import jax
import jax.numpy as jnp
from jax import lax

D = 8192
POLES = 8
TAPS = 3
TOKENS = 1024


def pole_rates(key):
    base = jax.random.fold_in(key, 101)
    share = 0.5
    pick = jax.random.uniform(jax.random.fold_in(base, 1), (D, POLES), jnp.float32)
    level = jax.random.uniform(jax.random.fold_in(base, 2), (D, POLES), jnp.float32)
    slow_low = math.log(0.1 * math.log(10.0) / TOKENS)
    slow_high = math.log(math.log(10.0) / TOKENS)
    fast_low = math.log(1.0 / 50.0)
    fast_high = math.log(1.0 / 30.0)
    slow = jnp.exp(slow_low + (slow_high - slow_low) * level)
    fast = jnp.exp(fast_low + (fast_high - fast_low) * level)
    return jnp.where(pick < share, slow, fast)


def draw_decay(key, part):
    return pole_rates(key).astype(jnp.float32)


def draw_residues(key, part):
    rates = pole_rates(key)
    normal_part = jax.random.truncated_normal(jax.random.fold_in(key, 23), -4.0, 4.0, (D, POLES), jnp.float32)
    return (normal_part * jnp.sqrt(2.0 * rates / POLES)).astype(jnp.float32)


def draw_state_in(key, part):
    rates = pole_rates(key)
    normal_part = jax.random.truncated_normal(jax.random.fold_in(key, 37), -4.0, 4.0, (D, POLES), jnp.float32)
    return (normal_part * jnp.sqrt(0.5 / rates)).astype(jnp.float32)


def levels(rng, dims, shards, smallest, top_value):
    gain, own = 1.0, jax.random.fold_in(rng, 6)
    for position, parts in shards:
        steps = jnp.exp(jax.random.uniform(jax.random.fold_in(own, position), (parts,), jnp.float32, smallest / len(shards), top_value / len(shards)))
        gain = gain * jnp.repeat(steps, dims[position] // parts).reshape([-1 if axis == position else 1 for axis in range(len(dims))])
    return gain


def centred(key, shape, spread, limit, cuts=(), kind=jnp.bfloat16):
    factor_of = levels(key, shape, cuts, -0.22, 0.18) if cuts else 1.0
    drawn = jax.random.normal(key, shape, jnp.float32) * spread * factor_of
    return jnp.minimum(jnp.maximum(drawn, -limit), limit).astype(kind)


def setup_inputs(seed: int = 0) -> dict:
    seeds = jax.random.split(jax.random.key(seed), 8)
    stream_in = centred(seeds[0], (TOKENS, D), 1.0, 6.0, ((0, 8), (1, 4)))
    features = centred(seeds[1], (3, TOKENS, D), 1.0, 6.0, ((1, 8), (2, 4)))
    conv_taps = centred(seeds[2], (3, TAPS, D), TAPS ** -0.5, 3.5, ((2, 4),), jnp.float32)
    decay = draw_decay(jax.random.fold_in(seeds[7], 71), 0)
    residues = draw_residues(jax.random.fold_in(seeds[7], 71), 0)
    state_in = draw_state_in(jax.random.fold_in(seeds[7], 71), 0)
    out_weight = centred(seeds[6], (D, D), D ** -0.5, 0.0625, ((0, 8), (1, 4)))
    return {"stream_in": stream_in, "features": features, "conv_taps": conv_taps, "decay": decay, "residues": residues, "state_in": state_in, "out_weight": out_weight}


def filter_group(pieces):
    mixed_in, rates, weights, initial = pieces
    block_len = mixed_in.shape[1]
    positions = jnp.arange(block_len).astype(jnp.float32)
    offsets = (jnp.arange(block_len)[:, None] - jnp.arange(block_len)[None, :]).astype(jnp.float32)
    lower = offsets >= 0.0
    clipped = jnp.maximum(offsets, 0.0)
    toeplitz = jnp.zeros((rates.shape[0], block_len, block_len), jnp.float32)
    for pole in range(rates.shape[1]):
        term = weights[:, pole, None, None] * jnp.exp(-rates[:, pole, None, None] * clipped[None])
        toeplitz = toeplitz + jnp.where(lower[None], term, 0.0)
    inner = jnp.einsum("gij,njg->nig", toeplitz, mixed_in, precision=lax.Precision.HIGHEST)
    carried = jnp.exp(-rates[:, :, None] * (block_len - positions))
    summary = jnp.einsum("njg,grj->ngr", mixed_in, carried, precision=lax.Precision.HIGHEST)
    step_decay = jnp.exp(-rates * block_len)

    def advance(state, term):
        return step_decay * state + term, state

    last_state, starts = lax.scan(advance, initial, summary)
    outward = weights[:, :, None] * jnp.exp(-rates[:, :, None] * positions)
    cross = jnp.einsum("ngr,gri->nig", starts, outward, precision=lax.Precision.HIGHEST)
    return inner + cross


def reference(stream_in, features, conv_taps, decay, residues, state_in, out_weight):
    feats = features.astype(jnp.float32)
    padded = jnp.pad(feats, ((0, 0), (TAPS - 1, 0), (0, 0)))
    shorted = jnp.zeros_like(feats)
    for tap in range(TAPS):
        shorted = shorted + conv_taps[:, tap, None, :] * padded[:, TAPS - 1 - tap:TAPS - 1 - tap + TOKENS, :]
    product = shorted[1] * shorted[2]
    block_len = min(128, TOKENS)
    block_count = TOKENS // block_len
    group = math.gcd(D, 512)
    group_count = D // group
    mixed_in = product.reshape(block_count, block_len, group_count, group).transpose(2, 0, 1, 3)
    filtered = lax.map(filter_group, (mixed_in, decay.reshape(group_count, group, POLES),
                                      residues.reshape(group_count, group, POLES),
                                      state_in.reshape(group_count, group, POLES)))
    filtered = filtered.transpose(1, 2, 0, 3).reshape(TOKENS, D)
    gated = (shorted[0] * filtered).astype(jnp.bfloat16)
    mixed = jnp.dot(gated, out_weight, preferred_element_type=jnp.float32)
    return (stream_in.astype(jnp.float32) + mixed).astype(jnp.bfloat16)
```

```python
import functools

import jax
import jax.numpy as jnp
from jax import lax
from jax.experimental import pallas as pl
from jax.experimental.pallas import tpu as pltpu
from jax.sharding import PartitionSpec as P


F32 = jnp.float32
BF16 = jnp.bfloat16
LANES = 128
SUBLANES = 8
PAD = 8


def widen(block_ref, halo_ref, buf):
    taps = halo_ref.shape[1]
    for plane in range(buf.shape[0]):
        lanes = slice(plane * LANES, (plane + 1) * LANES)
        buf[plane, PAD - taps : PAD, :] = halo_ref[0, :, lanes].astype(F32)
        buf[plane, PAD:, :] = block_ref[0, :, lanes].astype(F32)


class Convolved:
    def __init__(self, buf, taps, steps):
        self.buf, self.steps = buf, steps
        self.taps = [jnp.broadcast_to(tap, (SUBLANES, LANES)) for tap in taps]
        self.window = [self.row(-k) for k in range(len(taps) - 1, 0, -1)]

    def row(self, j):
        return self.buf[pl.ds(PAD + j, SUBLANES, stride=self.steps), :]

    def __call__(self, j):
        rows = self.window + [self.row(j)]
        self.window = rows[1:]
        total = self.taps[0] * rows[-1]
        for k in range(1, len(self.taps)):
            total = total + self.taps[k] * rows[-1 - k]
        return total


def taps_of(taps_ref, stream, lanes):
    return [taps_ref[stream, k : k + 1, lanes] for k in range(taps_ref.shape[1])]


def spread(row):
    return jnp.broadcast_to(row, (SUBLANES, LANES))


def states_kernel(k_ref, v_ref, hk_ref, hv_ref, taps_ref, decay_ref, end_ref, kb, vb):
    tokens, width = k_ref.shape[1:]
    poles = decay_ref.shape[0]
    steps = tokens // SUBLANES
    widen(k_ref, hk_ref, kb)
    widen(v_ref, hv_ref, vb)
    later = (SUBLANES - 1) - lax.broadcasted_iota(jnp.int32, (SUBLANES, LANES), 0)
    later = (later * steps).astype(F32)
    for plane in range(width // LANES):
        lanes = slice(plane * LANES, (plane + 1) * LANES)
        key = Convolved(kb.at[plane], taps_of(taps_ref, 1, lanes), steps)
        value = Convolved(vb.at[plane], taps_of(taps_ref, 2, lanes), steps)
        rates = [spread(decay_ref[r : r + 1, lanes]) for r in range(poles)]
        fades = [jnp.exp(-rate) for rate in rates]
        sums = None
        for j in range(steps):
            product = key(j) * value(j)
            if sums is None:
                sums = [product] * poles
            else:
                sums = [fades[r] * sums[r] + product for r in range(poles)]
        for r in range(poles):
            ended = fades[r] * sums[r] * jnp.exp(-rates[r] * later)
            end_ref[r : r + 1, lanes] = jnp.sum(ended, axis=0, keepdims=True)


def gated_kernel(
    half_ref, q_ref, k_ref, v_ref, hq_ref, hk_ref, hv_ref, taps_ref, decay_ref, residues_ref,
    state_ref, out_ref, qb, kb, vb, pb, ob,
):
    del half_ref
    tokens, width = k_ref.shape[1:]
    poles = decay_ref.shape[0]
    steps = tokens // SUBLANES
    widen(q_ref, hq_ref, qb)
    widen(k_ref, hk_ref, kb)
    widen(v_ref, hv_ref, vb)
    place = lax.broadcasted_iota(jnp.int32, (SUBLANES, LANES), 0)
    before = (place * steps).astype(F32)
    for plane in range(width // LANES):
        lanes = slice(plane * LANES, (plane + 1) * LANES)
        key = Convolved(kb.at[plane], taps_of(taps_ref, 1, lanes), steps)
        value = Convolved(vb.at[plane], taps_of(taps_ref, 2, lanes), steps)
        fades = [spread(jnp.exp(-decay_ref[r : r + 1, lanes])) for r in range(poles)]
        sums = None
        for j in range(steps):
            product = key(j) * value(j)
            pb[j] = product
            if sums is None:
                sums = [product] * poles
            else:
                sums = [fades[r] * sums[r] + product for r in range(poles)]
        for r in range(poles):
            rate = spread(decay_ref[r : r + 1, lanes])
            scan = fades[r] * sums[r]
            reach = 1
            while reach < SUBLANES:
                moved = jnp.where(place >= reach, pltpu.roll(scan, reach, 0), 0.0)
                scan = scan + jnp.exp(-rate * float(reach * steps)) * moved
                reach *= 2
            earlier = jnp.where(place >= 1, pltpu.roll(scan, 1, 0), 0.0)
            sums[r] = earlier + jnp.exp(-rate * before) * spread(state_ref[r : r + 1, lanes])
        query = Convolved(qb.at[plane], taps_of(taps_ref, 0, lanes), steps)
        weights = [spread(residues_ref[r : r + 1, lanes]) for r in range(poles)]
        for j in range(steps):
            product = pb[j]
            if j:
                sums = [fades[r] * sums[r] + product for r in range(poles)]
            else:
                sums = [sums[r] + product for r in range(poles)]
            terms = [weights[r] * sums[r] for r in range(poles)]
            while len(terms) > 1:
                terms = [a + b for a, b in zip(terms[::2], terms[1::2])] + terms[len(terms) & ~1 :]
            ob[pl.ds(j, SUBLANES, stride=steps), :] = query(j) * terms[0]
        out_ref[:, lanes] = ob[...].astype(out_ref.dtype)


def tile_of(count):
    return min(count, 512)


def end_states(features, halo, taps, rates):
    _, tokens, count = features.shape
    poles = rates.shape[0]
    width = tile_of(count)

    def part(array, stream):
        return pl.BlockSpec((1, array.shape[1], width), lambda i: (stream, 0, i))

    return pl.pallas_call(
        states_kernel,
        grid=(count // width,),
        in_specs=[part(features, 1), part(features, 2), part(halo, 1), part(halo, 2)]
        + [
            pl.BlockSpec(taps.shape[:2] + (width,), lambda i: (0, 0, i)),
            pl.BlockSpec((poles, width), lambda i: (0, i)),
        ],
        out_specs=pl.BlockSpec((poles, width), lambda i: (0, i)),
        out_shape=jax.ShapeDtypeStruct((poles, count), F32),
        scratch_shapes=[pltpu.VMEM((width // LANES, PAD + tokens, LANES), F32)] * 2,
        cost_estimate=pl.CostEstimate(
            flops=4 * poles * tokens * count, bytes_accessed=4 * tokens * count, transcendentals=0
        ),
        name="end_states",
    )(features, features, halo, halo, taps, rates)


def gated_half(half, share, features, halo, taps, rates, weights, state):
    _, tokens, _ = features.shape
    poles = rates.shape[0]
    width = tile_of(share)
    tiles = share // width

    def part(array, stream):
        return pl.BlockSpec(
            (1, array.shape[1], width), lambda i, half: (stream, 0, half[0] * tiles + i)
        )

    rows = pl.BlockSpec((poles, width), lambda i, half: (0, half[0] * tiles + i))
    return pl.pallas_call(
        gated_kernel,
        grid_spec=pltpu.PrefetchScalarGridSpec(
            num_scalar_prefetch=1,
            grid=(tiles,),
            in_specs=[part(features, i) for i in range(3)]
            + [part(halo, i) for i in range(3)]
            + [pl.BlockSpec(taps.shape[:2] + (width,), lambda i, half: (0, 0, half[0] * tiles + i))]
            + [rows] * 3,
            out_specs=pl.BlockSpec((tokens, width), lambda i, half: (0, i)),
            scratch_shapes=[pltpu.VMEM((width // LANES, PAD + tokens, LANES), F32)] * 3
            + [
                pltpu.VMEM((tokens // SUBLANES, SUBLANES, LANES), F32),
                pltpu.VMEM((tokens, LANES), F32),
            ],
        ),
        out_shape=jax.ShapeDtypeStruct((tokens, share), BF16),
        cost_estimate=pl.CostEstimate(
            flops=8 * poles * tokens * share, bytes_accessed=8 * tokens * share, transcendentals=0
        ),
        name="gated_half",
    )(half, features, features, features, halo, halo, halo, taps, rates, weights, state)


def shards(stream_in, features, conv_taps, decay, residues, state_in, out_weight):
    seqs, chans = lax.axis_size("seq"), lax.axis_size("chan")
    both = ("seq", "chan")
    lines = seqs // chans
    bits = chans.bit_length() - 1
    tokens = features.shape[1]
    share = out_weight.shape[0]
    here = lax.axis_index("seq")
    turned = [sum(((c >> i) & 1) << (bits - 1 - i) for i in range(bits)) for c in range(chans)]
    places = [(a, b, c) for a in range(chans) for b in range(lines) for c in range(chans)]

    def number(a, b, c):
        return (a * lines + b) * chans + c

    def moved(block, target):
        return lax.ppermute(block, both, [(number(*p), number(*target(*p))) for p in places])

    rates, weights, carried = decay.T, residues.T, state_in.T
    reach = conv_taps.shape[1] - 1
    halo = lax.ppermute(features[:, tokens - reach :, :], "seq", [(s, s + 1) for s in range(seqs - 1)])
    ends = end_states(features, halo, conv_taps, rates)
    state = jnp.exp(-rates * (here * tokens).astype(F32)) * carried
    for back in range(1, seqs):
        end = lax.ppermute(ends, "seq", [(s, s + back) for s in range(seqs - back)])
        state = state + jnp.exp(-rates * float((back - 1) * tokens)) * end

    own = here % lines
    order = list(range(1, lines)) + [0]
    slots = {}
    for j in order:
        half = ((own + j) % lines).astype(jnp.int32)[None]
        gated = gated_half(half, share, features, halo, conv_taps, rates, weights, state)
        slots[j] = [moved(gated, lambda a, b, c, j=j: (c, (b + j) % lines, turned[a ^ c]))]
    for i in range(bits):
        flip = 1 << (bits - 1 - i)
        for j in order:
            slots[j] = slots[j] + [moved(x, lambda a, b, c: (a, b, c ^ flip)) for x in slots[j]]

    total = stream_in.astype(F32)
    for slot in range(chans):
        mixed = jnp.dot(slots[0][slot], out_weight, preferred_element_type=F32)
        for j in range(1, lines):
            part = jnp.dot(slots[j][slot], out_weight, preferred_element_type=F32).astype(BF16)
            mixed = mixed + moved(part, lambda a, b, c: (a, (b - j) % lines, c)).astype(F32)
        mixed = moved(mixed.astype(BF16), lambda a, b, c: (a ^ turned[c] ^ slot, b, c))
        total = total + mixed.astype(F32)
    return total.astype(BF16)


def solution(mesh):
    return jax.shard_map(
        shards,
        mesh=mesh,
        in_specs=(
            P("seq", "chan"),
            P(None, "seq", "chan"),
            P(None, None, "chan"),
            P("chan", None),
            P("chan", None),
            P("chan", None),
            P("seq", "chan"),
        ),
        out_specs=P("seq", "chan"),
        check_vma=False,
    )
```

```python
import functools

import jax
import jax.numpy as jnp
from jax import lax
from jax.experimental import pallas as pl
from jax.experimental.pallas import tpu as pltpu
from jax.sharding import PartitionSpec as P


F32 = jnp.float32
BF16 = jnp.bfloat16
LANES = 128
SUBLANES = 8
PAD = 8
PIECES = 1


class Convolved:
    def __init__(self, block_ref, halo_ref, taps_ref, stream, lanes, buf):
        tokens, count = block_ref.shape[1], taps_ref.shape[1]
        if halo_ref is None:
            buf[:PAD, :] = jnp.zeros((PAD, LANES), F32)
        else:
            buf[PAD - count + 1 : PAD, :] = halo_ref[stream, :, lanes].astype(F32)
        buf[PAD:, :] = block_ref[stream, :, lanes].astype(F32)
        self.buf, self.steps = buf, tokens // SUBLANES
        self.taps = [spread(taps_ref[stream, k : k + 1, lanes]) for k in range(count)]
        self.window = [self.row(-k) for k in range(count - 1, 0, -1)]

    def row(self, j):
        return self.buf[pl.ds(PAD + j, SUBLANES, stride=self.steps), :]

    def __call__(self, j):
        rows = self.window + [self.row(j)]
        self.window = rows[1:]
        total = self.taps[0] * rows[-1]
        for k in range(1, len(self.taps)):
            total = total + self.taps[k] * rows[-1 - k]
        return total


def spread(row):
    return jnp.broadcast_to(row, (SUBLANES, LANES))


def over_planes(count, together, body):
    planes = count // LANES
    together = math_gcd(planes, together)

    def step(i, carry):
        for which in range(together):
            body(which, i * together + which)
        return carry

    lax.fori_loop(0, planes // together, step, 0)


def math_gcd(a, b):
    return a if b == 0 else math_gcd(b, a % b)


def lanes_at(plane, start=0):
    return pl.ds(pl.multiple_of(start + plane * LANES, LANES), LANES)


def states_kernel(
    block_hbm, taps_hbm, decay_hbm, residues_hbm, carried_hbm,
    end_ref, block_ref, taps_ref, decay_ref, residues_ref, carried_ref, kb, vb, sems,
):
    tokens, count = block_ref.shape[1:]
    poles = decay_ref.shape[0]
    steps = tokens // SUBLANES
    parts = sems.shape[0] - 5
    width = count // parts
    small = [
        pltpu.make_async_copy(source, target, sems.at[parts + i])
        for i, (source, target) in enumerate(
            [
                (taps_hbm, taps_ref),
                (decay_hbm, decay_ref),
                (residues_hbm, residues_ref),
                (carried_hbm, carried_ref),
                (block_hbm.at[:1], block_ref.at[:1]),
            ]
        )
    ]
    large = []
    for i in range(parts):
        lanes = pl.ds(i * width, width)
        large.append(
            pltpu.make_async_copy(
                block_hbm.at[1:, :, lanes], block_ref.at[1:, :, lanes], sems.at[i]
            )
        )
    for copy in large[:1] + small[:2] + large[1:] + small[2:]:
        copy.start()
    later = (SUBLANES - 1) - lax.broadcasted_iota(jnp.int32, (SUBLANES, LANES), 0)
    later = (later * steps + 1).astype(F32)

    def body(first, which, plane):
        lanes = lanes_at(plane, first)
        key = Convolved(block_ref, None, taps_ref, 1, lanes, kb.at[which])
        value = Convolved(block_ref, None, taps_ref, 2, lanes, vb.at[which])
        rates = [spread(decay_ref[r : r + 1, lanes]) for r in range(poles)]
        every = jnp.exp(-decay_ref[:, lanes])
        fades = [spread(every[r : r + 1]) for r in range(poles)]
        sums = None
        for j in range(steps):
            product = key(j) * value(j)
            if sums is None:
                sums = [product] * poles
            else:
                sums = [fades[r] * sums[r] + product for r in range(poles)]
        for r in range(poles):
            ended = sums[r] * jnp.exp(-rates[r] * later)
            end_ref[r : r + 1, lanes] = jnp.sum(ended, axis=0, keepdims=True)

    for copy in small[:2]:
        copy.wait()
    for i in range(parts):
        large[i].wait()
        over_planes(width, kb.shape[0], functools.partial(body, i * width))
    for copy in small[2:]:
        copy.wait()


def gated_kernel(
    j, lines, place_ref, block_ref, halo_ref, taps_ref, decay_ref, residues_ref,
    carried_ref, prefix_ref, last_ref, *refs,
):
    brought = []
    if len(refs) == 9:
        brought = [pltpu.make_async_copy(refs[0], refs[2], refs[-1])]
        refs = refs[1:2] + refs[3:-1]
    out_ref, qb, kb, vb, pb, ob = refs
    for copy in brought:
        copy.start()
    tokens, share = out_ref.shape
    poles = decay_ref.shape[0]
    steps = tokens // SUBLANES
    first = lax.rem(place_ref[0] + j, lines) * share
    since_start = (place_ref[0] * tokens).astype(F32)
    since_last = (place_ref[1] * tokens).astype(F32)
    upper = place_ref[1] != place_ref[0]
    place = lax.broadcasted_iota(jnp.int32, (SUBLANES, LANES), 0)
    before = (place * steps).astype(F32)

    def body(which, plane):
        lanes = lanes_at(plane, first)
        key = Convolved(block_ref, halo_ref, taps_ref, 1, lanes, kb.at[which])
        value = Convolved(block_ref, halo_ref, taps_ref, 2, lanes, vb.at[which])
        rates = decay_ref[:, lanes]
        every = jnp.exp(-rates)
        state = jnp.exp(-rates * since_start) * carried_ref[:, lanes] + prefix_ref[:, lanes]
        last = jnp.exp(-rates * since_last) * last_ref[:, lanes]
        state = state + jnp.where(upper, last, 0.0)
        fades = [spread(every[r : r + 1]) for r in range(poles)]
        sums = None
        for j in range(steps):
            product = key(j) * value(j)
            pb[which, j] = product
            if sums is None:
                sums = [product] * poles
            else:
                sums = [fades[r] * sums[r] + product for r in range(poles)]
        for r in range(poles):
            rate = spread(rates[r : r + 1])
            scan = fades[r] * sums[r]
            reach = 1
            while reach < SUBLANES:
                moved = jnp.where(place >= reach, pltpu.roll(scan, reach, 0), 0.0)
                scan = scan + jnp.exp(-rate * float(reach * steps)) * moved
                reach *= 2
            earlier = jnp.where(place >= 1, pltpu.roll(scan, 1, 0), 0.0)
            sums[r] = earlier + jnp.exp(-rate * before) * spread(state[r : r + 1])
        query = Convolved(block_ref, halo_ref, taps_ref, 0, lanes, qb.at[which])
        weights = [spread(residues_ref[r : r + 1, lanes]) for r in range(poles)]
        for j in range(steps):
            product = pb[which, j]
            if j:
                sums = [fades[r] * sums[r] + product for r in range(poles)]
            else:
                sums = [sums[r] + product for r in range(poles)]
            terms = [weights[r] * sums[r] for r in range(poles)]
            while len(terms) > 1:
                terms = [a + b for a, b in zip(terms[::2], terms[1::2])] + terms[len(terms) & ~1 :]
            ob[which, pl.ds(j, SUBLANES, stride=steps), :] = query(j) * terms[0]
        out_ref[:, lanes_at(plane)] = ob[which].astype(out_ref.dtype)

    over_planes(share, kb.shape[0], body)
    for copy in brought:
        copy.wait()


VMEM = pl.BlockSpec(memory_space=pltpu.VMEM)
SMEM = pl.BlockSpec(memory_space=pltpu.SMEM)
ROOM = pltpu.CompilerParams(vmem_limit_bytes=8 << 20)
TOGETHER = 2


def end_states(*arrays):
    features, _, rates = arrays[:3]
    _, tokens, count = features.shape
    poles = rates.shape[0]
    return pl.pallas_call(
        states_kernel,
        in_specs=[pl.BlockSpec(memory_space=pltpu.HBM)] * 5,
        out_specs=[VMEM] * 6,
        out_shape=[jax.ShapeDtypeStruct((poles, count), F32)]
        + [jax.ShapeDtypeStruct(array.shape, array.dtype) for array in arrays],
        scratch_shapes=[pltpu.VMEM((TOGETHER, PAD + tokens, LANES), F32)] * 2
        + [pltpu.SemaphoreType.DMA((math_gcd(count // LANES, 4) + 5,))],
        compiler_params=ROOM,
        cost_estimate=pl.CostEstimate(
            flops=4 * poles * tokens * count, bytes_accessed=6 * tokens * count, transcendentals=0
        ),
        name="end_states",
    )(*arrays)


def gated_half(j, lines, place, share, arrays, states, brought=()):
    tokens, poles = arrays[0].shape[1], states[0].shape[0]
    shapes = [jax.ShapeDtypeStruct((tokens, share), BF16)]
    shapes += [jax.ShapeDtypeStruct(array.shape, array.dtype) for array in brought]
    return pl.pallas_call(
        functools.partial(gated_kernel, j, lines),
        in_specs=[SMEM]
        + [VMEM] * (len(arrays) + len(states))
        + [pl.BlockSpec(memory_space=pltpu.HBM)] * len(brought),
        out_specs=[VMEM] * len(shapes),
        out_shape=shapes,
        scratch_shapes=[pltpu.VMEM((TOGETHER, PAD + tokens, LANES), F32)] * 3
        + [
            pltpu.VMEM((TOGETHER, tokens // SUBLANES, SUBLANES, LANES), F32),
            pltpu.VMEM((TOGETHER, tokens, LANES), F32),
        ]
        + [pltpu.SemaphoreType.DMA] * len(brought),
        compiler_params=ROOM,
        cost_estimate=pl.CostEstimate(
            flops=8 * poles * tokens * share, bytes_accessed=8 * tokens * share, transcendentals=0
        ),
        name="gated_half",
    )(place, *arrays, *states, *brought)


def shards(stream_in, features, conv_taps, decay, residues, state_in, out_weight):
    seqs, chans = lax.axis_size("seq"), lax.axis_size("chan")
    both = ("seq", "chan")
    lines = seqs // chans
    bits = chans.bit_length() - 1
    tokens = features.shape[1]
    share, columns = out_weight.shape
    here = lax.axis_index("seq")
    turned = [sum(((c >> i) & 1) << (bits - 1 - i) for i in range(bits)) for c in range(chans)]
    places = [(a, b, c) for a in range(chans) for b in range(lines) for c in range(chans)]

    def number(a, b, c):
        return (a * lines + b) * chans + c

    def moved(block, target):
        return lax.ppermute(block, both, [(number(*p), number(*target(*p))) for p in places])

    rates, weights, carried = decay.T, residues.T, state_in.T
    reach = conv_taps.shape[1] - 1
    halo = lax.ppermute(
        features[:, tokens - reach :, :], "seq", [(s, s + 1) for s in range(seqs - 1)]
    )
    ends, features, conv_taps, rates, weights, carried = end_states(
        features, conv_taps, rates, weights, carried
    )
    ends = ends + first_tokens(features[1:, :reach], halo[1:], conv_taps[1:], rates, tokens)
    prefix = jnp.zeros_like(ends)
    width = 1
    while True:
        other = lax.ppermute(ends, "seq", [(s, s ^ width) for s in range(seqs)])
        if 2 * width >= seqs:
            break
        upper = (here & width) != 0
        within = (here % width * tokens).astype(F32)
        fade = jnp.exp(-rates * float(width * tokens))
        prefix = prefix + jnp.where(upper, jnp.exp(-rates * within) * other, 0.0)
        ends = jnp.where(upper, ends + fade * other, other + fade * ends)
        width *= 2

    order = list(range(1, lines)) + [0]
    place = jnp.stack([here, here % width]).astype(jnp.int32)
    slots = {}
    for j in order:
        gated, *rest = gated_half(
            j, lines, place, share, (features, halo, conv_taps, rates, weights),
            (carried, prefix, other), [out_weight] if j == order[-1] else [],
        )
        slots[j] = [moved(gated, lambda a, b, c, j=j: (c, (b + j) % lines, turned[a ^ c]))]
    out_weight = rest[0]
    for i in range(bits):
        flip = 1 << (bits - 1 - i)
        for j in order:
            for slot in range(1 << i):
                slots[j].append(moved(slots[j][slot], lambda a, b, c: (a, b, c ^ flip)))

    pieces = math_gcd(PIECES, columns // LANES)
    size = columns // pieces
    totals = [stream_in[:, p * size : (p + 1) * size].astype(F32) for p in range(pieces)]
    for slot in range(chans):
        for p in range(pieces):
            weight = out_weight[:, p * size : (p + 1) * size]
            mixed = jnp.dot(slots[0][slot], weight, preferred_element_type=F32)
            for j in range(1, lines):
                part = jnp.dot(slots[j][slot], weight, preferred_element_type=F32).astype(BF16)
                part = moved(part, lambda a, b, c: (a, (b - j) % lines, c))
                mixed = mixed + part.astype(F32)
            mixed = moved(mixed.astype(BF16), lambda a, b, c: (a ^ turned[c] ^ slot, b, c))
            totals[p] = totals[p] + mixed.astype(F32)
    return jnp.concatenate([total.astype(BF16) for total in totals], axis=1)


def first_tokens(features, halo, taps, rates, tokens):
    features, halo = features.astype(F32), halo.astype(F32)
    reach = halo.shape[1]
    total = jnp.zeros_like(rates)
    for t in range(reach):
        inner = sum(taps[:, k] * features[:, t - k] for k in range(t + 1))
        outer = sum(taps[:, k] * halo[:, reach + t - k] for k in range(t + 1, reach + 1))
        change = inner[0] * outer[1] + outer[0] * (inner[1] + outer[1])
        total = total + jnp.exp(-rates * float(tokens - t)) * change
    return total


def solution(mesh):
    return jax.shard_map(
        shards,
        mesh=mesh,
        in_specs=(
            P("seq", "chan"),
            P(None, "seq", "chan"),
            P(None, None, "chan"),
            P("chan", None),
            P("chan", None),
            P("chan", None),
            P("seq", "chan"),
        ),
        out_specs=P("seq", "chan"),
        check_vma=False,
    )
```

```python
import functools

import jax
import jax.numpy as jnp
from jax import lax
from jax.experimental import pallas as pl
from jax.experimental.pallas import tpu as pltpu
from jax.sharding import PartitionSpec as P


F32 = jnp.float32
BF16 = jnp.bfloat16
LANES = 128
SUBLANES = 8
PAD = 8


class Convolved:
    def __init__(self, block_ref, halo_ref, taps_ref, stream, lanes, buf):
        tokens, count = block_ref.shape[1], taps_ref.shape[1]
        if halo_ref is None:
            buf[:PAD, :] = jnp.zeros((PAD, LANES), F32)
        else:
            buf[PAD - count + 1 : PAD, :] = halo_ref[stream, :, lanes].astype(F32)
        buf[PAD:, :] = block_ref[stream, :, lanes].astype(F32)
        self.buf, self.steps = buf, tokens // SUBLANES
        self.taps = [spread(taps_ref[stream, k : k + 1, lanes]) for k in range(count)]
        self.window = [self.row(-k) for k in range(count - 1, 0, -1)]

    def row(self, j):
        return self.buf[pl.ds(PAD + j, SUBLANES, stride=self.steps), :]

    def __call__(self, j):
        rows = self.window + [self.row(j)]
        self.window = rows[1:]
        total = self.taps[0] * rows[-1]
        for k in range(1, len(self.taps)):
            total = total + self.taps[k] * rows[-1 - k]
        return total


def spread(row):
    return jnp.broadcast_to(row, (SUBLANES, LANES))


def over_planes(count, together, body):
    planes = count // LANES
    together = math_gcd(planes, together)

    def step(i, carry):
        for which in range(together):
            body(which, i * together + which)
        return carry

    lax.fori_loop(0, planes // together, step, 0)


def math_gcd(a, b):
    return a if b == 0 else math_gcd(b, a % b)


def lanes_at(plane, start=0):
    return pl.ds(pl.multiple_of(start + plane * LANES, LANES), LANES)


def states_kernel(
    block_hbm, taps_hbm, decay_hbm, residues_hbm, carried_hbm,
    end_ref, block_ref, taps_ref, decay_ref, residues_ref, carried_ref, kb, vb, sems,
):
    tokens, count = block_ref.shape[1:]
    poles = decay_ref.shape[0]
    steps = tokens // SUBLANES
    parts = sems.shape[0] - 5
    width = count // parts
    small = [
        pltpu.make_async_copy(source, target, sems.at[parts + i])
        for i, (source, target) in enumerate(
            [
                (taps_hbm, taps_ref),
                (decay_hbm, decay_ref),
                (residues_hbm, residues_ref),
                (carried_hbm, carried_ref),
                (block_hbm.at[:1], block_ref.at[:1]),
            ]
        )
    ]
    large = []
    for i in range(parts):
        lanes = pl.ds(i * width, width)
        large.append(
            pltpu.make_async_copy(
                block_hbm.at[1:, :, lanes], block_ref.at[1:, :, lanes], sems.at[i]
            )
        )
    for copy in large[:1] + small[:2] + large[1:] + small[2:]:
        copy.start()
    later = (SUBLANES - 1) - lax.broadcasted_iota(jnp.int32, (SUBLANES, LANES), 0)
    later = (later * steps + 1).astype(F32)

    def body(first, which, plane):
        lanes = lanes_at(plane, first)
        key = Convolved(block_ref, None, taps_ref, 1, lanes, kb.at[which])
        value = Convolved(block_ref, None, taps_ref, 2, lanes, vb.at[which])
        rates = [spread(decay_ref[r : r + 1, lanes]) for r in range(poles)]
        every = jnp.exp(-decay_ref[:, lanes])
        fades = [spread(every[r : r + 1]) for r in range(poles)]
        sums = None
        for j in range(steps):
            product = key(j) * value(j)
            if sums is None:
                sums = [product] * poles
            else:
                sums = [fades[r] * sums[r] + product for r in range(poles)]
        for r in range(poles):
            ended = sums[r] * jnp.exp(-rates[r] * later)
            end_ref[r : r + 1, lanes] = jnp.sum(ended, axis=0, keepdims=True)

    for copy in small[:2]:
        copy.wait()
    for i in range(parts):
        large[i].wait()
        over_planes(width, kb.shape[0], functools.partial(body, i * width))
    for copy in small[2:]:
        copy.wait()


def gated_kernel(
    j, lines, parts, place_ref, block_ref, halo_ref, taps_ref, decay_ref, residues_ref,
    carried_ref, prefix_ref, last_ref, *refs,
):
    *out_refs, qb, kb, vb, pb, ob = refs[len(refs) - parts - 5 :]
    tokens, share = block_ref.shape[1], out_refs[0].shape[1]
    poles = decay_ref.shape[0]
    steps = tokens // SUBLANES
    first = lax.rem(place_ref[0] + j, lines) * share
    since_start = (place_ref[0] * tokens).astype(F32)
    since_last = (place_ref[1] * tokens).astype(F32)
    upper = place_ref[1] != place_ref[0]
    place = lax.broadcasted_iota(jnp.int32, (SUBLANES, LANES), 0)
    before = (place * steps).astype(F32)

    def body(which, plane):
        lanes = lanes_at(plane, first)
        key = Convolved(block_ref, halo_ref, taps_ref, 1, lanes, kb.at[which])
        value = Convolved(block_ref, halo_ref, taps_ref, 2, lanes, vb.at[which])
        rates = decay_ref[:, lanes]
        every = jnp.exp(-rates)
        state = jnp.exp(-rates * since_start) * carried_ref[:, lanes] + prefix_ref[:, lanes]
        last = jnp.exp(-rates * since_last) * last_ref[:, lanes]
        state = state + jnp.where(upper, last, 0.0)
        fades = [spread(every[r : r + 1]) for r in range(poles)]
        sums = None
        for j in range(steps):
            product = key(j) * value(j)
            pb[which, j] = product
            if sums is None:
                sums = [product] * poles
            else:
                sums = [fades[r] * sums[r] + product for r in range(poles)]
        for r in range(poles):
            rate = spread(rates[r : r + 1])
            scan = fades[r] * sums[r]
            reach = 1
            while reach < SUBLANES:
                moved = jnp.where(place >= reach, pltpu.roll(scan, reach, 0), 0.0)
                scan = scan + jnp.exp(-rate * float(reach * steps)) * moved
                reach *= 2
            earlier = jnp.where(place >= 1, pltpu.roll(scan, 1, 0), 0.0)
            sums[r] = earlier + jnp.exp(-rate * before) * spread(state[r : r + 1])
        query = Convolved(block_ref, halo_ref, taps_ref, 0, lanes, qb.at[which])
        weights = [spread(residues_ref[r : r + 1, lanes]) for r in range(poles)]
        for j in range(steps):
            product = pb[which, j]
            if j:
                sums = [fades[r] * sums[r] + product for r in range(poles)]
            else:
                sums = [sums[r] + product for r in range(poles)]
            terms = [weights[r] * sums[r] for r in range(poles)]
            while len(terms) > 1:
                terms = [a + b for a, b in zip(terms[::2], terms[1::2])] + terms[len(terms) & ~1 :]
            ob[which, pl.ds(j, SUBLANES, stride=steps), :] = query(j) * terms[0]
        for i, out_ref in enumerate(out_refs):
            rows = out_ref.shape[0]
            part = ob[which, i * rows : (i + 1) * rows]
            out_ref[:, lanes_at(plane)] = part.astype(out_ref.dtype)

    over_planes(share, kb.shape[0], body)


VMEM = pl.BlockSpec(memory_space=pltpu.VMEM)
SMEM = pl.BlockSpec(memory_space=pltpu.SMEM)
ROOM = pltpu.CompilerParams(vmem_limit_bytes=8 << 20)
TOGETHER = 2


def end_states(*arrays):
    features, _, rates = arrays[:3]
    _, tokens, count = features.shape
    poles = rates.shape[0]
    return pl.pallas_call(
        states_kernel,
        in_specs=[pl.BlockSpec(memory_space=pltpu.HBM)] * 5,
        out_specs=[VMEM] * 6,
        out_shape=[jax.ShapeDtypeStruct((poles, count), F32)]
        + [jax.ShapeDtypeStruct(array.shape, array.dtype) for array in arrays],
        scratch_shapes=[pltpu.VMEM((TOGETHER, PAD + tokens, LANES), F32)] * 2
        + [pltpu.SemaphoreType.DMA((math_gcd(count // LANES, 4) + 5,))],
        compiler_params=ROOM,
        cost_estimate=pl.CostEstimate(
            flops=4 * poles * tokens * count, bytes_accessed=6 * tokens * count, transcendentals=0
        ),
        name="end_states",
    )(*arrays)


def gated_half(j, lines, parts, place, share, arrays, states, brought=()):
    tokens, poles = arrays[0].shape[1], states[0].shape[0]
    shapes = [jax.ShapeDtypeStruct((tokens // parts, share), BF16)] * parts
    return pl.pallas_call(
        functools.partial(gated_kernel, j, lines, parts),
        in_specs=[SMEM]
        + [VMEM] * (len(arrays) + len(states) + len(brought)),
        out_specs=[VMEM] * len(shapes),
        out_shape=shapes,
        scratch_shapes=[pltpu.VMEM((TOGETHER, PAD + tokens, LANES), F32)] * 3
        + [
            pltpu.VMEM((TOGETHER, tokens // SUBLANES, SUBLANES, LANES), F32),
            pltpu.VMEM((TOGETHER, tokens, LANES), F32),
        ],
        compiler_params=ROOM,
        cost_estimate=pl.CostEstimate(
            flops=8 * poles * tokens * share, bytes_accessed=8 * tokens * share, transcendentals=0
        ),
        name="gated_half",
    )(place, *arrays, *states, *brought)


def shards(stream_in, features, conv_taps, decay, residues, state_in, out_weight):
    seqs, chans = lax.axis_size("seq"), lax.axis_size("chan")
    both = ("seq", "chan")
    lines = seqs // chans
    bits = chans.bit_length() - 1
    tokens = features.shape[1]
    share, _ = out_weight.shape
    here = lax.axis_index("seq")
    turned = [sum(((c >> i) & 1) << (bits - 1 - i) for i in range(bits)) for c in range(chans)]
    places = [(a, b, c) for a in range(chans) for b in range(lines) for c in range(chans)]

    def number(a, b, c):
        return (a * lines + b) * chans + c

    def moved(block, target):
        return lax.ppermute(block, both, [(number(*p), number(*target(*p))) for p in places])

    rates, weights, carried = decay.T, residues.T, state_in.T
    reach = conv_taps.shape[1] - 1
    halo = lax.ppermute(
        features[:, tokens - reach :, :], "seq", [(s, s + 1) for s in range(seqs - 1)]
    )
    ends, features, conv_taps, rates, weights, carried = end_states(
        features, conv_taps, rates, weights, carried
    )
    ends = ends + first_tokens(features[1:, :reach], halo[1:], conv_taps[1:], rates, tokens)
    prefix = jnp.zeros_like(ends)
    width = 1
    while True:
        other = lax.ppermute(ends, "seq", [(s, s ^ width) for s in range(seqs)])
        if 2 * width >= seqs:
            break
        upper = (here & width) != 0
        within = (here % width * tokens).astype(F32)
        fade = jnp.exp(-rates * float(width * tokens))
        prefix = prefix + jnp.where(upper, jnp.exp(-rates * within) * other, 0.0)
        ends = jnp.where(upper, ends + fade * other, other + fade * ends)
        width *= 2

    order = list(range(1, lines)) + [0]
    place = jnp.stack([here, here % width]).astype(jnp.int32)
    top = chans >> 1
    blocks = {}
    for j in order:
        results = gated_half(
            j, lines, 2 if j else 1, place, share, (features, halo, conv_taps, rates, weights),
            (carried, prefix, other), [],
        )
        blocks[j] = [moved(results[0], lambda a, b, c: (c, (b + j) % lines, turned[a ^ c]))]
        if j:
            other_half = moved(results[1], lambda a, b, c: (a, b, c ^ top))
            blocks[j].append(
                moved(other_half, lambda a, b, c: (c ^ top, (b + j) % lines, turned[a ^ c ^ top]))
            )

    odd = lax.axis_index("chan") % 2 == 1
    pieces = {}
    for j in order:
        lower = [jnp.concatenate(blocks[j], axis=0) if len(blocks[j]) > 1 else blocks[j][0]]
        sides = {}

        def beside(slot):
            return moved(lower[slot], lambda a, b, c: (a, b, c ^ 1))

        sides[0] = beside(0)
        for i in range(bits - 1):
            flip = top >> i
            for slot in range(1 << i):
                new = slot + (1 << i)
                lower.append(moved(lower[slot], lambda a, b, c: (a, b, c ^ flip)))
                sides[new] = beside(new)
        for slot in range(top):
            for group, pair in enumerate([(lower[slot], sides[slot]), (sides[slot], lower[slot])]):
                pieces[j, group, slot] = product_of(jnp.where(odd, *pair), out_weight, j)

    half = tokens // 2
    totals = [stream_in[p * half : (p + 1) * half].astype(F32) for p in range(2)]
    for group in range(2):
        for slot in range(top):
            cut = group == 0 and slot == 0
            own = [pieces[0, group, slot]]
            if cut:
                own = lax.optimization_barrier((own[0][:half], own[0][half:]))
            for p in range(2 if cut else 1):
                start = p * half
                stop = start + (half if cut else tokens)
                mixed = own[p]
                for j in range(1, lines):
                    part = moved(
                        pieces[j, group, slot][start:stop], lambda a, b, c: (a, (b - j) % lines, c)
                    )
                    mixed = mixed + part.astype(F32)

                def target(a, b, c):
                    return a ^ turned[c] ^ (slot + top * (c % 2 == group)), b, c

                mixed = moved(mixed.astype(BF16), target)
                for i in [p] if cut else [0, 1]:
                    part = mixed if cut else mixed[i * half : (i + 1) * half]
                    totals[i] = totals[i] + part.astype(F32)
    return jnp.concatenate([total.astype(BF16) for total in totals], axis=0)


def product_of(block, weight, j):
    product = jnp.dot(block, weight, preferred_element_type=F32)
    return product.astype(BF16) if j else lax.optimization_barrier(product)


def first_tokens(features, halo, taps, rates, tokens):
    features, halo = features.astype(F32), halo.astype(F32)
    reach = halo.shape[1]
    total = jnp.zeros_like(rates)
    for t in range(reach):
        inner = sum(taps[:, k] * features[:, t - k] for k in range(t + 1))
        outer = sum(taps[:, k] * halo[:, reach + t - k] for k in range(t + 1, reach + 1))
        change = inner[0] * outer[1] + outer[0] * (inner[1] + outer[1])
        total = total + jnp.exp(-rates * float(tokens - t)) * change
    return total


def solution(mesh):
    return jax.shard_map(
        shards,
        mesh=mesh,
        in_specs=(
            P("seq", "chan"),
            P(None, "seq", "chan"),
            P(None, None, "chan"),
            P("chan", None),
            P("chan", None),
            P("chan", None),
            P("seq", "chan"),
        ),
        out_specs=P("seq", "chan"),
        check_vma=False,
    )
```

```python
import functools

import jax
import jax.numpy as jnp
from jax import lax
from jax.experimental import pallas as pl
from jax.experimental.pallas import tpu as pltpu
from jax.sharding import PartitionSpec as P


F32 = jnp.float32
BF16 = jnp.bfloat16
LANES = 128
SUBLANES = 8
PAD = 8


class Convolved:
    def __init__(self, block_ref, halo_ref, taps_ref, stream, lanes, buf):
        tokens, count = block_ref.shape[1], taps_ref.shape[1]
        if halo_ref is None:
            buf[:PAD, :] = jnp.zeros((PAD, LANES), F32)
        else:
            buf[PAD - count + 1 : PAD, :] = halo_ref[stream, :, lanes].astype(F32)
        buf[PAD:, :] = block_ref[stream, :, lanes].astype(F32)
        self.buf, self.steps = buf, tokens // SUBLANES
        self.taps = [spread(taps_ref[stream, k : k + 1, lanes]) for k in range(count)]
        self.window = [self.row(-k) for k in range(count - 1, 0, -1)]

    def row(self, j):
        return self.buf[pl.ds(PAD + j, SUBLANES, stride=self.steps), :]

    def __call__(self, j):
        rows = self.window + [self.row(j)]
        self.window = rows[1:]
        total = self.taps[0] * rows[-1]
        for k in range(1, len(self.taps)):
            total = total + self.taps[k] * rows[-1 - k]
        return total


def spread(row):
    return jnp.broadcast_to(row, (SUBLANES, LANES))


def over_planes(count, together, body):
    planes = count // LANES
    together = math_gcd(planes, together)

    def step(i, carry):
        for which in range(together):
            body(which, i * together + which)
        return carry

    lax.fori_loop(0, planes // together, step, 0)


def math_gcd(a, b):
    return a if b == 0 else math_gcd(b, a % b)


def lanes_at(plane, start=0):
    return pl.ds(pl.multiple_of(start + plane * LANES, LANES), LANES)


def states_kernel(
    block_hbm, taps_hbm, decay_hbm, residues_hbm, carried_hbm,
    end_ref, block_ref, taps_ref, decay_ref, residues_ref, carried_ref, kb, vb, sems,
):
    tokens, count = block_ref.shape[1:]
    poles = decay_ref.shape[0]
    steps = tokens // SUBLANES
    parts = sems.shape[0] - 5
    width = count // parts
    small = [
        pltpu.make_async_copy(source, target, sems.at[parts + i])
        for i, (source, target) in enumerate(
            [
                (taps_hbm, taps_ref),
                (decay_hbm, decay_ref),
                (residues_hbm, residues_ref),
                (carried_hbm, carried_ref),
                (block_hbm.at[:1], block_ref.at[:1]),
            ]
        )
    ]
    large = []
    for i in range(parts):
        lanes = pl.ds(i * width, width)
        large.append(
            pltpu.make_async_copy(
                block_hbm.at[1:, :, lanes], block_ref.at[1:, :, lanes], sems.at[i]
            )
        )
    for copy in large[:1] + small[:2] + large[1:] + small[2:]:
        copy.start()
    later = (SUBLANES - 1) - lax.broadcasted_iota(jnp.int32, (SUBLANES, LANES), 0)
    later = (later * steps + 1).astype(F32)

    def body(first, which, plane):
        lanes = lanes_at(plane, first)
        key = Convolved(block_ref, None, taps_ref, 1, lanes, kb.at[which])
        value = Convolved(block_ref, None, taps_ref, 2, lanes, vb.at[which])
        rates = [spread(decay_ref[r : r + 1, lanes]) for r in range(poles)]
        every = jnp.exp(-decay_ref[:, lanes])
        fades = [spread(every[r : r + 1]) for r in range(poles)]
        sums = None
        for j in range(steps):
            product = key(j) * value(j)
            if sums is None:
                sums = [product] * poles
            else:
                sums = [fades[r] * sums[r] + product for r in range(poles)]
        for r in range(poles):
            ended = sums[r] * jnp.exp(-rates[r] * later)
            end_ref[r : r + 1, lanes] = jnp.sum(ended, axis=0, keepdims=True)

    for copy in small[:2]:
        copy.wait()
    for i in range(parts):
        large[i].wait()
        over_planes(width, kb.shape[0], functools.partial(body, i * width))
    for copy in small[2:]:
        copy.wait()


def gated_kernel(
    j, lines, parts, place_ref, block_ref, halo_ref, taps_ref, decay_ref, residues_ref,
    carried_ref, prefix_ref, last_ref, *refs,
):
    *out_refs, qb, kb, vb, pb, ob = refs[len(refs) - parts - 5 :]
    tokens, share = block_ref.shape[1], out_refs[0].shape[1]
    poles = decay_ref.shape[0]
    steps = tokens // SUBLANES
    first = lax.rem(place_ref[0] + j, lines) * share
    since_start = (place_ref[0] * tokens).astype(F32)
    since_last = (place_ref[1] * tokens).astype(F32)
    upper = place_ref[1] != place_ref[0]
    place = lax.broadcasted_iota(jnp.int32, (SUBLANES, LANES), 0)
    before = (place * steps).astype(F32)

    def body(which, plane):
        lanes = lanes_at(plane, first)
        key = Convolved(block_ref, halo_ref, taps_ref, 1, lanes, kb.at[which])
        value = Convolved(block_ref, halo_ref, taps_ref, 2, lanes, vb.at[which])
        rates = decay_ref[:, lanes]
        every = jnp.exp(-rates)
        state = jnp.exp(-rates * since_start) * carried_ref[:, lanes] + prefix_ref[:, lanes]
        last = jnp.exp(-rates * since_last) * last_ref[:, lanes]
        state = state + jnp.where(upper, last, 0.0)
        fades = [spread(every[r : r + 1]) for r in range(poles)]
        sums = None
        for j in range(steps):
            product = key(j) * value(j)
            pb[which, j] = product
            if sums is None:
                sums = [product] * poles
            else:
                sums = [fades[r] * sums[r] + product for r in range(poles)]
        for r in range(poles):
            rate = spread(rates[r : r + 1])
            scan = fades[r] * sums[r]
            reach = 1
            while reach < SUBLANES:
                moved = jnp.where(place >= reach, pltpu.roll(scan, reach, 0), 0.0)
                scan = scan + jnp.exp(-rate * float(reach * steps)) * moved
                reach *= 2
            earlier = jnp.where(place >= 1, pltpu.roll(scan, 1, 0), 0.0)
            sums[r] = earlier + jnp.exp(-rate * before) * spread(state[r : r + 1])
        query = Convolved(block_ref, halo_ref, taps_ref, 0, lanes, qb.at[which])
        weights = [spread(residues_ref[r : r + 1, lanes]) for r in range(poles)]
        for j in range(steps):
            product = pb[which, j]
            if j:
                sums = [fades[r] * sums[r] + product for r in range(poles)]
            else:
                sums = [sums[r] + product for r in range(poles)]
            terms = [weights[r] * sums[r] for r in range(poles)]
            while len(terms) > 1:
                terms = [a + b for a, b in zip(terms[::2], terms[1::2])] + terms[len(terms) & ~1 :]
            ob[which, pl.ds(j, SUBLANES, stride=steps), :] = query(j) * terms[0]
        for i, out_ref in enumerate(out_refs):
            rows = out_ref.shape[0]
            part = ob[which, i * rows : (i + 1) * rows]
            out_ref[:, lanes_at(plane)] = part.astype(out_ref.dtype)

    over_planes(share, kb.shape[0], body)


VMEM = pl.BlockSpec(memory_space=pltpu.VMEM)
SMEM = pl.BlockSpec(memory_space=pltpu.SMEM)
ROOM = pltpu.CompilerParams(vmem_limit_bytes=8 << 20)
TOGETHER = 2


def end_states(*arrays):
    features, _, rates = arrays[:3]
    _, tokens, count = features.shape
    poles = rates.shape[0]
    return pl.pallas_call(
        states_kernel,
        in_specs=[pl.BlockSpec(memory_space=pltpu.HBM)] * 5,
        out_specs=[VMEM] * 6,
        out_shape=[jax.ShapeDtypeStruct((poles, count), F32)]
        + [jax.ShapeDtypeStruct(array.shape, array.dtype) for array in arrays],
        scratch_shapes=[pltpu.VMEM((TOGETHER, PAD + tokens, LANES), F32)] * 2
        + [pltpu.SemaphoreType.DMA((math_gcd(count // LANES, 4) + 5,))],
        compiler_params=ROOM,
        cost_estimate=pl.CostEstimate(
            flops=4 * poles * tokens * count, bytes_accessed=6 * tokens * count, transcendentals=0
        ),
        name="end_states",
    )(*arrays)


def gated_half(j, lines, parts, place, share, arrays, states, brought=()):
    tokens, poles = arrays[0].shape[1], states[0].shape[0]
    shapes = [jax.ShapeDtypeStruct((tokens // parts, share), BF16)] * parts
    return pl.pallas_call(
        functools.partial(gated_kernel, j, lines, parts),
        in_specs=[SMEM]
        + [VMEM] * (len(arrays) + len(states) + len(brought)),
        out_specs=[VMEM] * len(shapes),
        out_shape=shapes,
        scratch_shapes=[pltpu.VMEM((TOGETHER, PAD + tokens, LANES), F32)] * 3
        + [
            pltpu.VMEM((TOGETHER, tokens // SUBLANES, SUBLANES, LANES), F32),
            pltpu.VMEM((TOGETHER, tokens, LANES), F32),
        ],
        compiler_params=ROOM,
        cost_estimate=pl.CostEstimate(
            flops=8 * poles * tokens * share, bytes_accessed=8 * tokens * share, transcendentals=0
        ),
        name="gated_half",
    )(place, *arrays, *states, *brought)


def shards(stream_in, features, conv_taps, decay, residues, state_in, out_weight):
    seqs, chans = lax.axis_size("seq"), lax.axis_size("chan")
    both = ("seq", "chan")
    lines = seqs // chans
    bits = chans.bit_length() - 1
    tokens = features.shape[1]
    share, _ = out_weight.shape
    here = lax.axis_index("seq")
    turned = [sum(((c >> i) & 1) << (bits - 1 - i) for i in range(bits)) for c in range(chans)]
    places = [(a, b, c) for a in range(chans) for b in range(lines) for c in range(chans)]

    def number(a, b, c):
        return (a * lines + b) * chans + c

    def moved(block, target):
        return lax.ppermute(block, both, [(number(*p), number(*target(*p))) for p in places])

    rates, weights, carried = decay.T, residues.T, state_in.T
    reach = conv_taps.shape[1] - 1
    halo = lax.ppermute(
        features[:, tokens - reach :, :], "seq", [(s, s + 1) for s in range(seqs - 1)]
    )
    ends, features, conv_taps, rates, weights, carried = end_states(
        features, conv_taps, rates, weights, carried
    )
    ends = ends + first_tokens(features[1:, :reach], halo[1:], conv_taps[1:], rates, tokens)
    prefix = jnp.zeros_like(ends)
    width = 1
    while True:
        other = lax.ppermute(ends, "seq", [(s, s ^ width) for s in range(seqs)])
        if 2 * width >= seqs:
            break
        upper = (here & width) != 0
        within = (here % width * tokens).astype(F32)
        fade = jnp.exp(-rates * float(width * tokens))
        prefix = prefix + jnp.where(upper, jnp.exp(-rates * within) * other, 0.0)
        ends = jnp.where(upper, ends + fade * other, other + fade * ends)
        width *= 2

    order = list(range(1, lines)) + [0]
    place = jnp.stack([here, here % width]).astype(jnp.int32)
    top = chans >> 1
    blocks = {}
    for j in order:
        results = gated_half(
            j, lines, 2 if j else 1, place, share, (features, halo, conv_taps, rates, weights),
            (carried, prefix, other), [],
        )
        blocks[j] = [moved(results[0], lambda a, b, c: (c, (b + j) % lines, turned[a ^ c]))]
        if j:
            other_half = moved(results[1], lambda a, b, c: (a, b, c ^ top))
            blocks[j].append(
                moved(other_half, lambda a, b, c: (c ^ top, (b + j) % lines, turned[a ^ c ^ top]))
            )

    odd = lax.axis_index("chan") % 2 == 1
    pieces = {}
    for j in order:
        lower, sides = [], []
        for p, block in enumerate(blocks[j]):
            lower.append(block)
            sides.append(moved(block, lambda a, b, c: (a, b, c ^ 1)))
            if j:
                pieces[j, 0, 0, p] = product_of(jnp.where(odd, lower[p], sides[p]), out_weight, j)
        if len(lower) > 1:
            lower, sides = [jnp.concatenate(lower, axis=0)], [jnp.concatenate(sides, axis=0)]
        for i in range(bits - 1):
            flip = top >> i
            for slot in range(1 << i):
                new = slot + (1 << i)
                lower.append(moved(lower[slot], lambda a, b, c: (a, b, c ^ flip)))
                sides.append(moved(lower[new], lambda a, b, c: (a, b, c ^ 1)))
        for slot in range(top):
            for group, pair in enumerate([(lower[slot], sides[slot]), (sides[slot], lower[slot])]):
                if (j, group, slot, 0) not in pieces:
                    pieces[j, group, slot, 0] = product_of(jnp.where(odd, *pair), out_weight, j)

    half = tokens // 2
    total = stream_in.astype(F32)
    for group in range(2):
        for slot in range(top):
            cut = group == 0 and slot == 0
            own = [pieces[0, group, slot, 0]]
            if cut:
                own = lax.optimization_barrier((own[0][:half], own[0][half:]))
            came = []
            for p, mixed in enumerate(own):
                for j in range(1, lines):
                    part = moved(pieces[j, group, slot, p], lambda a, b, c: (a, (b - j) % lines, c))
                    mixed = mixed + part.astype(F32)

                def target(a, b, c):
                    return a ^ turned[c] ^ (slot + top * (c % 2 == group)), b, c

                came.append(moved(mixed.astype(BF16), target))
            total = total + (jnp.concatenate(came, axis=0) if cut else came[0]).astype(F32)
    return total.astype(BF16)


def product_of(block, weight, j):
    product = jnp.dot(block, weight, preferred_element_type=F32)
    return product.astype(BF16) if j else lax.optimization_barrier(product)


def first_tokens(features, halo, taps, rates, tokens):
    features, halo = features.astype(F32), halo.astype(F32)
    reach = halo.shape[1]
    total = jnp.zeros_like(rates)
    for t in range(reach):
        inner = sum(taps[:, k] * features[:, t - k] for k in range(t + 1))
        outer = sum(taps[:, k] * halo[:, reach + t - k] for k in range(t + 1, reach + 1))
        change = inner[0] * outer[1] + outer[0] * (inner[1] + outer[1])
        total = total + jnp.exp(-rates * float(tokens - t)) * change
    return total


def solution(mesh):
    return jax.shard_map(
        shards,
        mesh=mesh,
        in_specs=(
            P("seq", "chan"),
            P(None, "seq", "chan"),
            P(None, None, "chan"),
            P("chan", None),
            P("chan", None),
            P("chan", None),
            P("seq", "chan"),
        ),
        out_specs=P("seq", "chan"),
        check_vma=False,
    )
```

```python
import functools

import jax
import jax.numpy as jnp
from jax import lax
from jax.experimental import pallas as pl
from jax.experimental.pallas import tpu as pltpu
from jax.sharding import PartitionSpec as P


F32 = jnp.float32
BF16 = jnp.bfloat16
LANES = 128
SUBLANES = 8
PAD = 8


class Convolved:
    def __init__(self, block_ref, halo_ref, taps_ref, stream, lanes, buf):
        tokens, count = block_ref.shape[1], taps_ref.shape[1]
        if halo_ref is None:
            buf[:PAD, :] = jnp.zeros((PAD, LANES), F32)
        else:
            buf[PAD - count + 1 : PAD, :] = halo_ref[stream, :, lanes].astype(F32)
        buf[PAD:, :] = block_ref[stream, :, lanes].astype(F32)
        self.buf, self.steps = buf, tokens // SUBLANES
        self.taps = [spread(taps_ref[stream, k : k + 1, lanes]) for k in range(count)]
        self.window = [self.row(-k) for k in range(count - 1, 0, -1)]

    def row(self, j):
        return self.buf[pl.ds(PAD + j, SUBLANES, stride=self.steps), :]

    def __call__(self, j):
        rows = self.window + [self.row(j)]
        self.window = rows[1:]
        total = self.taps[0] * rows[-1]
        for k in range(1, len(self.taps)):
            total = total + self.taps[k] * rows[-1 - k]
        return total


def spread(row):
    return jnp.broadcast_to(row, (SUBLANES, LANES))


def over_planes(count, together, body):
    planes = count // LANES
    together = math_gcd(planes, together)

    def step(i, carry):
        for which in range(together):
            body(which, i * together + which)
        return carry

    lax.fori_loop(0, planes // together, step, 0)


def math_gcd(a, b):
    return a if b == 0 else math_gcd(b, a % b)


def lanes_at(plane, start=0):
    return pl.ds(pl.multiple_of(start + plane * LANES, LANES), LANES)


def states_kernel(
    block_hbm, taps_hbm, small_hbm, end_ref, block_ref, taps_ref, small_ref, kb, vb, sems
):
    tokens, count = block_ref.shape[1:]
    poles = end_ref.shape[0]
    decay_ref = small_ref.at[0]
    steps = tokens // SUBLANES
    parts = sems.shape[0] - 3
    width = count // parts
    small = [
        pltpu.make_async_copy(source, target, sems.at[parts + i])
        for i, (source, target) in enumerate(
            [
                (taps_hbm, taps_ref),
                (small_hbm, small_ref),
                (block_hbm.at[:1], block_ref.at[:1]),
            ]
        )
    ]
    large = []
    for i in range(parts):
        lanes = pl.ds(i * width, width)
        large.append(
            pltpu.make_async_copy(
                block_hbm.at[1:, :, lanes], block_ref.at[1:, :, lanes], sems.at[i]
            )
        )
    for copy in large[:1] + small[:2] + large[1:] + small[2:]:
        copy.start()
    later = (SUBLANES - 1) - lax.broadcasted_iota(jnp.int32, (SUBLANES, LANES), 0)
    later = (later * steps + 1).astype(F32)

    def body(first, which, plane):
        lanes = lanes_at(plane, first)
        key = Convolved(block_ref, None, taps_ref, 1, lanes, kb.at[which])
        value = Convolved(block_ref, None, taps_ref, 2, lanes, vb.at[which])
        rates = [spread(decay_ref[r : r + 1, lanes]) for r in range(poles)]
        every = jnp.exp(-decay_ref[:, lanes])
        fades = [spread(every[r : r + 1]) for r in range(poles)]
        sums = None
        for j in range(steps):
            product = key(j) * value(j)
            if sums is None:
                sums = [product] * poles
            else:
                sums = [fades[r] * sums[r] + product for r in range(poles)]
        for r in range(poles):
            ended = sums[r] * jnp.exp(-rates[r] * later)
            end_ref[r : r + 1, lanes] = jnp.sum(ended, axis=0, keepdims=True)

    for copy in small[:2]:
        copy.wait()
    for i in range(parts):
        large[i].wait()
        over_planes(width, kb.shape[0], functools.partial(body, i * width))
    for copy in small[2:]:
        copy.wait()


def gated_kernel(
    j, lines, parts, place_ref, block_ref, halo_ref, taps_ref, small_ref, prefix_ref, last_ref, *refs
):
    *out_refs, qb, kb, vb, pb, ob = refs[len(refs) - parts - 5 :]
    tokens, share = block_ref.shape[1], out_refs[0].shape[1]
    poles = prefix_ref.shape[0]
    decay_ref, residues_ref, carried_ref = (small_ref.at[i] for i in range(3))
    steps = tokens // SUBLANES
    first = lax.rem(place_ref[0] + j, lines) * share
    since_start = (place_ref[0] * tokens).astype(F32)
    since_last = (place_ref[1] * tokens).astype(F32)
    upper = place_ref[1] != place_ref[0]
    place = lax.broadcasted_iota(jnp.int32, (SUBLANES, LANES), 0)
    before = (place * steps).astype(F32)

    def body(which, plane):
        lanes = lanes_at(plane, first)
        key = Convolved(block_ref, halo_ref, taps_ref, 1, lanes, kb.at[which])
        value = Convolved(block_ref, halo_ref, taps_ref, 2, lanes, vb.at[which])
        rates = decay_ref[:, lanes]
        every = jnp.exp(-rates)
        state = jnp.exp(-rates * since_start) * carried_ref[:, lanes] + prefix_ref[:, lanes]
        last = jnp.exp(-rates * since_last) * last_ref[:, lanes]
        state = state + jnp.where(upper, last, 0.0)
        fades = [spread(every[r : r + 1]) for r in range(poles)]
        sums = None
        for j in range(steps):
            product = key(j) * value(j)
            pb[which, j] = product
            if sums is None:
                sums = [product] * poles
            else:
                sums = [fades[r] * sums[r] + product for r in range(poles)]
        for r in range(poles):
            rate = spread(rates[r : r + 1])
            scan = fades[r] * sums[r]
            reach = 1
            while reach < SUBLANES:
                moved = jnp.where(place >= reach, pltpu.roll(scan, reach, 0), 0.0)
                scan = scan + jnp.exp(-rate * float(reach * steps)) * moved
                reach *= 2
            earlier = jnp.where(place >= 1, pltpu.roll(scan, 1, 0), 0.0)
            sums[r] = earlier + jnp.exp(-rate * before) * spread(state[r : r + 1])
        query = Convolved(block_ref, halo_ref, taps_ref, 0, lanes, qb.at[which])
        weights = [spread(residues_ref[r : r + 1, lanes]) for r in range(poles)]
        for j in range(steps):
            product = pb[which, j]
            if j:
                sums = [fades[r] * sums[r] + product for r in range(poles)]
            else:
                sums = [sums[r] + product for r in range(poles)]
            terms = [weights[r] * sums[r] for r in range(poles)]
            while len(terms) > 1:
                terms = [a + b for a, b in zip(terms[::2], terms[1::2])] + terms[len(terms) & ~1 :]
            ob[which, pl.ds(j, SUBLANES, stride=steps), :] = query(j) * terms[0]
        for i, out_ref in enumerate(out_refs):
            rows = out_ref.shape[0]
            part = ob[which, i * rows : (i + 1) * rows]
            out_ref[:, lanes_at(plane)] = part.astype(out_ref.dtype)

    over_planes(share, kb.shape[0], body)


VMEM = pl.BlockSpec(memory_space=pltpu.VMEM)
SMEM = pl.BlockSpec(memory_space=pltpu.SMEM)
ROOM = pltpu.CompilerParams(vmem_limit_bytes=8 << 20)
TOGETHER = 2


def end_states(*arrays):
    features, _, small = arrays
    _, tokens, count = features.shape
    poles = small.shape[1]
    return pl.pallas_call(
        states_kernel,
        in_specs=[pl.BlockSpec(memory_space=pltpu.HBM)] * 3,
        out_specs=[VMEM] * 4,
        out_shape=[jax.ShapeDtypeStruct((poles, count), F32)]
        + [jax.ShapeDtypeStruct(array.shape, array.dtype) for array in arrays],
        scratch_shapes=[pltpu.VMEM((TOGETHER, PAD + tokens, LANES), F32)] * 2
        + [pltpu.SemaphoreType.DMA((math_gcd(count // LANES, 4) + 3,))],
        compiler_params=ROOM,
        cost_estimate=pl.CostEstimate(
            flops=4 * poles * tokens * count, bytes_accessed=6 * tokens * count, transcendentals=0
        ),
        name="end_states",
    )(*arrays)


def gated_half(j, lines, parts, place, share, arrays, states, brought=()):
    tokens, poles = arrays[0].shape[1], states[0].shape[0]
    shapes = [jax.ShapeDtypeStruct((tokens // parts, share), BF16)] * parts
    return pl.pallas_call(
        functools.partial(gated_kernel, j, lines, parts),
        in_specs=[SMEM]
        + [VMEM] * (len(arrays) + len(states) + len(brought)),
        out_specs=[VMEM] * len(shapes),
        out_shape=shapes,
        scratch_shapes=[pltpu.VMEM((TOGETHER, PAD + tokens, LANES), F32)] * 3
        + [
            pltpu.VMEM((TOGETHER, tokens // SUBLANES, SUBLANES, LANES), F32),
            pltpu.VMEM((TOGETHER, tokens, LANES), F32),
        ],
        compiler_params=ROOM,
        cost_estimate=pl.CostEstimate(
            flops=8 * poles * tokens * share, bytes_accessed=8 * tokens * share, transcendentals=0
        ),
        name="gated_half",
    )(place, *arrays, *states, *brought)


def shards(stream_in, features, conv_taps, decay, residues, state_in, out_weight):
    seqs, chans = lax.axis_size("seq"), lax.axis_size("chan")
    both = ("seq", "chan")
    lines = seqs // chans
    bits = chans.bit_length() - 1
    tokens = features.shape[1]
    share, _ = out_weight.shape
    here = lax.axis_index("seq")
    turned = [sum(((c >> i) & 1) << (bits - 1 - i) for i in range(bits)) for c in range(chans)]
    places = [(a, b, c) for a in range(chans) for b in range(lines) for c in range(chans)]

    def number(a, b, c):
        return (a * lines + b) * chans + c

    def moved(block, target):
        return lax.ppermute(block, both, [(number(*p), number(*target(*p))) for p in places])

    reach = conv_taps.shape[1] - 1
    halo = lax.ppermute(
        features[:, tokens - reach :, :], "seq", [(s, s + 1) for s in range(seqs - 1)]
    )
    small = jnp.stack([decay.T, residues.T, state_in.T])
    ends, features, conv_taps, small = end_states(features, conv_taps, small)
    rates = small[0]
    ends = ends + first_tokens(features[1:, :reach], halo[1:], conv_taps[1:], rates, tokens)
    prefix = jnp.zeros_like(ends)
    width = 1
    while True:
        other = lax.ppermute(ends, "seq", [(s, s ^ width) for s in range(seqs)])
        if 2 * width >= seqs:
            break
        upper = (here & width) != 0
        within = (here % width * tokens).astype(F32)
        fade = jnp.exp(-rates * float(width * tokens))
        prefix = prefix + jnp.where(upper, jnp.exp(-rates * within) * other, 0.0)
        ends = jnp.where(upper, ends + fade * other, other + fade * ends)
        width *= 2

    order = list(range(1, lines)) + [0]
    place = jnp.stack([here, here % width]).astype(jnp.int32)
    top = chans >> 1
    blocks = {}
    for j in order:
        results = gated_half(
            j, lines, 2 if j else 1, place, share, (features, halo, conv_taps, small),
            (prefix, other), [],
        )
        blocks[j] = [moved(results[0], lambda a, b, c: (c, (b + j) % lines, turned[a ^ c]))]
        if j:
            other_half = moved(results[1], lambda a, b, c: (a, b, c ^ top))
            blocks[j].append(
                moved(other_half, lambda a, b, c: (c ^ top, (b + j) % lines, turned[a ^ c ^ top]))
            )

    odd = lax.axis_index("chan") % 2 == 1
    pieces = {}
    for j in order:
        lower, sides = [], []
        for p, block in enumerate(blocks[j]):
            lower.append(block)
            sides.append(moved(block, lambda a, b, c: (a, b, c ^ 1)))
            if j:
                pieces[j, 0, 0, p] = product_of(jnp.where(odd, lower[p], sides[p]), out_weight, j)
        if len(lower) > 1:
            lower, sides = [jnp.concatenate(lower, axis=0)], [jnp.concatenate(sides, axis=0)]
        for i in range(bits - 1):
            flip = top >> i
            for slot in range(1 << i):
                new = slot + (1 << i)
                lower.append(moved(lower[slot], lambda a, b, c: (a, b, c ^ flip)))
                sides.append(moved(lower[new], lambda a, b, c: (a, b, c ^ 1)))
        for slot in range(top):
            for group, pair in enumerate([(lower[slot], sides[slot]), (sides[slot], lower[slot])]):
                if (j, group, slot, 0) not in pieces:
                    pieces[j, group, slot, 0] = product_of(jnp.where(odd, *pair), out_weight, j)

    half = tokens // 2
    total = stream_in.astype(F32)
    for group in range(2):
        for slot in range(top):
            cut = group == 0 and slot == 0
            own = [pieces[0, group, slot, 0]]
            if cut:
                own = lax.optimization_barrier((own[0][:half], own[0][half:]))
            came = []
            for p, mixed in enumerate(own):
                for j in range(1, lines):
                    part = moved(pieces[j, group, slot, p], lambda a, b, c: (a, (b - j) % lines, c))
                    mixed = mixed + part.astype(F32)

                def target(a, b, c):
                    return a ^ turned[c] ^ (slot + top * (c % 2 == group)), b, c

                came.append(moved(mixed.astype(BF16), target))
            total = total + (jnp.concatenate(came, axis=0) if cut else came[0]).astype(F32)
    return total.astype(BF16)


def product_of(block, weight, j):
    product = jnp.dot(block, weight, preferred_element_type=F32)
    return product.astype(BF16) if j else lax.optimization_barrier(product)


def first_tokens(features, halo, taps, rates, tokens):
    features, halo = features.astype(F32), halo.astype(F32)
    reach = halo.shape[1]
    total = jnp.zeros_like(rates)
    for t in range(reach):
        inner = sum(taps[:, k] * features[:, t - k] for k in range(t + 1))
        outer = sum(taps[:, k] * halo[:, reach + t - k] for k in range(t + 1, reach + 1))
        change = inner[0] * outer[1] + outer[0] * (inner[1] + outer[1])
        total = total + jnp.exp(-rates * float(tokens - t)) * change
    return total


def solution(mesh):
    return jax.shard_map(
        shards,
        mesh=mesh,
        in_specs=(
            P("seq", "chan"),
            P(None, "seq", "chan"),
            P(None, None, "chan"),
            P("chan", None),
            P("chan", None),
            P("chan", None),
            P("seq", "chan"),
        ),
        out_specs=P("seq", "chan"),
        check_vma=False,
    )
```

```python
import functools

import jax
import jax.numpy as jnp
from jax import lax
from jax.experimental import pallas as pl
from jax.experimental.pallas import tpu as pltpu
from jax.sharding import PartitionSpec as P


F32 = jnp.float32
BF16 = jnp.bfloat16
LANES = 128
SUBLANES = 8
PAD = 8


class Convolved:
    def __init__(self, block_ref, halo_ref, taps_ref, stream, lanes, buf):
        tokens, count = block_ref.shape[1], taps_ref.shape[1]
        if halo_ref is None:
            buf[:PAD, :] = jnp.zeros((PAD, LANES), F32)
        else:
            buf[PAD - count + 1 : PAD, :] = halo_ref[stream, :, lanes].astype(F32)
        buf[PAD:, :] = block_ref[stream, :, lanes].astype(F32)
        self.buf, self.steps = buf, tokens // SUBLANES
        self.taps = [spread(taps_ref[stream, k : k + 1, lanes]) for k in range(count)]
        self.window = [self.row(-k) for k in range(count - 1, 0, -1)]

    def row(self, j):
        return self.buf[pl.ds(PAD + j, SUBLANES, stride=self.steps), :]

    def __call__(self, j):
        rows = self.window + [self.row(j)]
        self.window = rows[1:]
        total = self.taps[0] * rows[-1]
        for k in range(1, len(self.taps)):
            total = total + self.taps[k] * rows[-1 - k]
        return total


def spread(row):
    return jnp.broadcast_to(row, (SUBLANES, LANES))


def over_planes(count, together, body):
    planes = count // LANES
    together = math_gcd(planes, together)

    def step(i, carry):
        for which in range(together):
            body(which, i * together + which)
        return carry

    lax.fori_loop(0, planes // together, step, 0)


def math_gcd(a, b):
    return a if b == 0 else math_gcd(b, a % b)


def lanes_at(plane, start=0):
    return pl.ds(pl.multiple_of(start + plane * LANES, LANES), LANES)


def states_kernel(
    block_hbm, taps_hbm, small_hbm, end_ref, block_ref, taps_ref, small_ref, kb, vb, sems
):
    tokens, count = block_ref.shape[1:]
    poles = end_ref.shape[0]
    decay_ref = small_ref.at[0]
    steps = tokens // SUBLANES
    parts = sems.shape[0] - 3
    width = count // parts
    small = [
        pltpu.make_async_copy(source, target, sems.at[parts + i])
        for i, (source, target) in enumerate(
            [
                (taps_hbm, taps_ref),
                (small_hbm, small_ref),
                (block_hbm.at[:1], block_ref.at[:1]),
            ]
        )
    ]
    large = []
    for i in range(parts):
        lanes = pl.ds(i * width, width)
        large.append(
            pltpu.make_async_copy(
                block_hbm.at[1:, :, lanes], block_ref.at[1:, :, lanes], sems.at[i]
            )
        )
    for copy in large[:1] + small[:2] + large[1:] + small[2:]:
        copy.start()
    later = (SUBLANES - 1) - lax.broadcasted_iota(jnp.int32, (SUBLANES, LANES), 0)
    later = (later * steps + 1).astype(F32)

    def body(first, which, plane):
        lanes = lanes_at(plane, first)
        key = Convolved(block_ref, None, taps_ref, 1, lanes, kb.at[which])
        value = Convolved(block_ref, None, taps_ref, 2, lanes, vb.at[which])
        rates = [spread(decay_ref[r : r + 1, lanes]) for r in range(poles)]
        every = jnp.exp(-decay_ref[:, lanes])
        fades = [spread(every[r : r + 1]) for r in range(poles)]
        sums = None
        for j in range(steps):
            product = key(j) * value(j)
            if sums is None:
                sums = [product] * poles
            else:
                sums = [fades[r] * sums[r] + product for r in range(poles)]
        for r in range(poles):
            ended = sums[r] * jnp.exp(-rates[r] * later)
            end_ref[r : r + 1, lanes] = jnp.sum(ended, axis=0, keepdims=True)

    for copy in small[:2]:
        copy.wait()
    for i in range(parts):
        large[i].wait()
        over_planes(width, kb.shape[0], functools.partial(body, i * width))
    for copy in small[2:]:
        copy.wait()


def gated_kernel(
    j, lines, parts, place_ref, block_ref, halo_ref, taps_ref, small_ref, prefix_ref, last_ref, *refs
):
    *out_refs, qb, kb, vb, pb, ob = refs[len(refs) - parts - 5 :]
    tokens, share = block_ref.shape[1], out_refs[0].shape[1]
    poles = prefix_ref.shape[0]
    decay_ref, residues_ref, carried_ref = (small_ref.at[i] for i in range(3))
    steps = tokens // SUBLANES
    first = lax.rem(place_ref[0] + j, lines) * share
    since_start = (place_ref[0] * tokens).astype(F32)
    since_last = (place_ref[1] * tokens).astype(F32)
    upper = place_ref[1] != place_ref[0]
    place = lax.broadcasted_iota(jnp.int32, (SUBLANES, LANES), 0)
    before = (place * steps).astype(F32)

    def body(which, plane):
        lanes = lanes_at(plane, first)
        key = Convolved(block_ref, halo_ref, taps_ref, 1, lanes, kb.at[which])
        value = Convolved(block_ref, halo_ref, taps_ref, 2, lanes, vb.at[which])
        rates = decay_ref[:, lanes]
        every = jnp.exp(-rates)
        state = jnp.exp(-rates * since_start) * carried_ref[:, lanes] + prefix_ref[:, lanes]
        last = jnp.exp(-rates * since_last) * last_ref[:, lanes]
        state = state + jnp.where(upper, last, 0.0)
        fades = [spread(every[r : r + 1]) for r in range(poles)]
        sums = None
        for j in range(steps):
            product = key(j) * value(j)
            pb[which, j] = product
            if sums is None:
                sums = [product] * poles
            else:
                sums = [fades[r] * sums[r] + product for r in range(poles)]
        for r in range(poles):
            rate = spread(rates[r : r + 1])
            scan = fades[r] * sums[r]
            reach = 1
            while reach < SUBLANES:
                moved = jnp.where(place >= reach, pltpu.roll(scan, reach, 0), 0.0)
                scan = scan + jnp.exp(-rate * float(reach * steps)) * moved
                reach *= 2
            earlier = jnp.where(place >= 1, pltpu.roll(scan, 1, 0), 0.0)
            sums[r] = earlier + jnp.exp(-rate * before) * spread(state[r : r + 1])
        query = Convolved(block_ref, halo_ref, taps_ref, 0, lanes, qb.at[which])
        weights = [spread(residues_ref[r : r + 1, lanes]) for r in range(poles)]
        for j in range(steps):
            product = pb[which, j]
            if j:
                sums = [fades[r] * sums[r] + product for r in range(poles)]
            else:
                sums = [sums[r] + product for r in range(poles)]
            terms = [weights[r] * sums[r] for r in range(poles)]
            while len(terms) > 1:
                terms = [a + b for a, b in zip(terms[::2], terms[1::2])] + terms[len(terms) & ~1 :]
            ob[which, pl.ds(j, SUBLANES, stride=steps), :] = query(j) * terms[0]
        for i, out_ref in enumerate(out_refs):
            rows = out_ref.shape[0]
            part = ob[which, i * rows : (i + 1) * rows]
            out_ref[:, lanes_at(plane)] = part.astype(out_ref.dtype)

    over_planes(share, kb.shape[0], body)


VMEM = pl.BlockSpec(memory_space=pltpu.VMEM)
SMEM = pl.BlockSpec(memory_space=pltpu.SMEM)
ROOM = pltpu.CompilerParams(vmem_limit_bytes=8 << 20)
TOGETHER = 2


def end_states(*arrays):
    features, _, small = arrays
    _, tokens, count = features.shape
    poles = small.shape[1]
    return pl.pallas_call(
        states_kernel,
        in_specs=[pl.BlockSpec(memory_space=pltpu.HBM)] * 3,
        out_specs=[VMEM] * 4,
        out_shape=[jax.ShapeDtypeStruct((poles, count), F32)]
        + [jax.ShapeDtypeStruct(array.shape, array.dtype) for array in arrays],
        scratch_shapes=[pltpu.VMEM((TOGETHER, PAD + tokens, LANES), F32)] * 2
        + [pltpu.SemaphoreType.DMA((math_gcd(count // LANES, 4) + 3,))],
        compiler_params=ROOM,
        cost_estimate=pl.CostEstimate(
            flops=4 * poles * tokens * count, bytes_accessed=6 * tokens * count, transcendentals=0
        ),
        name="end_states",
    )(*arrays)


def gated_half(j, lines, parts, place, share, arrays, states, brought=()):
    tokens, poles = arrays[0].shape[1], states[0].shape[0]
    shapes = [jax.ShapeDtypeStruct((tokens // parts, share), BF16)] * parts
    return pl.pallas_call(
        functools.partial(gated_kernel, j, lines, parts),
        in_specs=[SMEM]
        + [VMEM] * (len(arrays) + len(states) + len(brought)),
        out_specs=[VMEM] * len(shapes),
        out_shape=shapes,
        scratch_shapes=[pltpu.VMEM((TOGETHER, PAD + tokens, LANES), F32)] * 3
        + [
            pltpu.VMEM((TOGETHER, tokens // SUBLANES, SUBLANES, LANES), F32),
            pltpu.VMEM((TOGETHER, tokens, LANES), F32),
        ],
        compiler_params=ROOM,
        cost_estimate=pl.CostEstimate(
            flops=8 * poles * tokens * share, bytes_accessed=8 * tokens * share, transcendentals=0
        ),
        name="gated_half",
    )(place, *arrays, *states, *brought)


def shards(stream_in, features, conv_taps, decay, residues, state_in, out_weight):
    seqs, chans = lax.axis_size("seq"), lax.axis_size("chan")
    both = ("seq", "chan")
    lines = seqs // chans
    bits = chans.bit_length() - 1
    tokens = features.shape[1]
    share, _ = out_weight.shape
    here = lax.axis_index("seq")
    turned = [sum(((c >> i) & 1) << (bits - 1 - i) for i in range(bits)) for c in range(chans)]
    places = [(a, b, c) for a in range(chans) for b in range(lines) for c in range(chans)]

    def number(a, b, c):
        return (a * lines + b) * chans + c

    def moved(block, target):
        return lax.ppermute(block, both, [(number(*p), number(*target(*p))) for p in places])

    reach = conv_taps.shape[1] - 1
    halo = lax.ppermute(
        features[:, tokens - reach :, :], "seq", [(s, s + 1) for s in range(seqs - 1)]
    )
    small = jnp.stack([decay.T, residues.T, state_in.T])
    ends, features, conv_taps, small = end_states(features, conv_taps, small)
    rates = small[0]
    ends = ends + first_tokens(features[1:, :reach], halo[1:], conv_taps[1:], rates, tokens)
    prefix = jnp.zeros_like(ends)
    width = 1
    while True:
        other = lax.ppermute(ends, "seq", [(s, s ^ width) for s in range(seqs)])
        if 2 * width >= seqs:
            break
        upper = (here & width) != 0
        within = (here % width * tokens).astype(F32)
        fade = jnp.exp(-rates * float(width * tokens))
        prefix = prefix + jnp.where(upper, jnp.exp(-rates * within) * other, 0.0)
        ends = jnp.where(upper, ends + fade * other, other + fade * ends)
        width *= 2

    order = list(range(1, lines)) + [0]
    place = jnp.stack([here, here % width]).astype(jnp.int32)
    top = chans >> 1
    blocks = {}
    for j in order:
        results = gated_half(
            j, lines, 2 if j else 1, place, share, (features, halo, conv_taps, small),
            (prefix, other), [],
        )
        blocks[j] = [moved(results[0], lambda a, b, c: (c, (b + j) % lines, turned[a ^ c]))]
        if j:
            other_half = moved(results[1], lambda a, b, c: (a, b, c ^ top))
            blocks[j].append(
                moved(other_half, lambda a, b, c: (c ^ top, (b + j) % lines, turned[a ^ c ^ top]))
            )

    odd = lax.axis_index("chan") % 2 == 1
    pieces = {}
    for j in order:
        lower, sides = [], []
        for p, block in enumerate(blocks[j]):
            lower.append(block)
            sides.append(moved(block, lambda a, b, c: (a, b, c ^ 1)))
            if j:
                pieces[j, 0, 0, p] = product_of(jnp.where(odd, lower[p], sides[p]), out_weight, j)
        if len(lower) > 1:
            lower, sides = [jnp.concatenate(lower, axis=0)], [jnp.concatenate(sides, axis=0)]
        for i in range(bits - 1):
            flip = top >> i
            for slot in range(1 << i):
                new = slot + (1 << i)
                lower.append(moved(lower[slot], lambda a, b, c: (a, b, c ^ flip)))
                sides.append(moved(lower[new], lambda a, b, c: (a, b, c ^ 1)))
        for slot in range(top):
            for group, pair in enumerate([(lower[slot], sides[slot]), (sides[slot], lower[slot])]):
                if (j, group, slot, 0) not in pieces:
                    pieces[j, group, slot, 0] = product_of(jnp.where(odd, *pair), out_weight, j)

    half = tokens // 2
    total = stream_in.astype(F32)
    for group in range(2):
        for slot in range(top):
            cut = group == 1 or slot == 0
            own = [pieces[0, group, slot, 0]]
            if cut:
                own = lax.optimization_barrier((own[0][:half], own[0][half:]))
            came = []
            for p, mixed in enumerate(own):
                for j in range(1, lines):
                    if group:
                        part = pieces[j, group, slot, 0][p * half : (p + 1) * half]
                    else:
                        part = pieces[j, group, slot, p]
                    part = moved(part, lambda a, b, c: (a, (b - j) % lines, c))
                    mixed = mixed + part.astype(F32)
                    mixed = mixed.astype(BF16) if j == lines - 1 else mixed

                def target(a, b, c):
                    return a ^ turned[c] ^ (slot + top * (c % 2 == group)), b, c

                came.append(moved(mixed, target))
            total = total + (jnp.concatenate(came, axis=0) if cut else came[0]).astype(F32)
    return total.astype(BF16)


def product_of(block, weight, j):
    product = jnp.dot(block, weight, preferred_element_type=F32)
    return product.astype(BF16) if j else lax.optimization_barrier(product)


def first_tokens(features, halo, taps, rates, tokens):
    features, halo = features.astype(F32), halo.astype(F32)
    reach = halo.shape[1]
    total = jnp.zeros_like(rates)
    for t in range(reach):
        inner = sum(taps[:, k] * features[:, t - k] for k in range(t + 1))
        outer = sum(taps[:, k] * halo[:, reach + t - k] for k in range(t + 1, reach + 1))
        change = inner[0] * outer[1] + outer[0] * (inner[1] + outer[1])
        total = total + jnp.exp(-rates * float(tokens - t)) * change
    return total


def solution(mesh):
    return jax.shard_map(
        shards,
        mesh=mesh,
        in_specs=(
            P("seq", "chan"),
            P(None, "seq", "chan"),
            P(None, None, "chan"),
            P("chan", None),
            P("chan", None),
            P("chan", None),
            P("seq", "chan"),
        ),
        out_specs=P("seq", "chan"),
        check_vma=False,
    )
```

```python
import functools

import jax
import jax.numpy as jnp
from jax import lax
from jax.experimental import pallas as pl
from jax.experimental.pallas import tpu as pltpu
from jax.sharding import PartitionSpec as P


F32 = jnp.float32
BF16 = jnp.bfloat16
LANES = 128
SUBLANES = 8
PAD = 8


class Convolved:
    def __init__(self, block_ref, halo_ref, taps_ref, stream, lanes, buf):
        tokens, count = block_ref.shape[1], taps_ref.shape[1]
        if halo_ref is None:
            buf[:PAD, :] = jnp.zeros((PAD, LANES), F32)
        else:
            buf[PAD - count + 1 : PAD, :] = halo_ref[stream, :, lanes].astype(F32)
        buf[PAD:, :] = block_ref[stream, :, lanes].astype(F32)
        self.buf, self.steps = buf, tokens // SUBLANES
        self.taps = [spread(taps_ref[stream, k : k + 1, lanes]) for k in range(count)]
        self.window = [self.row(-k) for k in range(count - 1, 0, -1)]

    def row(self, j):
        return self.buf[pl.ds(PAD + j, SUBLANES, stride=self.steps), :]

    def __call__(self, j):
        rows = self.window + [self.row(j)]
        self.window = rows[1:]
        total = self.taps[0] * rows[-1]
        for k in range(1, len(self.taps)):
            total = total + self.taps[k] * rows[-1 - k]
        return total


def spread(row):
    return jnp.broadcast_to(row, (SUBLANES, LANES))


def over_planes(count, together, body):
    planes = count // LANES
    together = math_gcd(planes, together)

    def step(i, carry):
        for which in range(together):
            body(which, i * together + which)
        return carry

    lax.fori_loop(0, planes // together, step, 0)


def math_gcd(a, b):
    return a if b == 0 else math_gcd(b, a % b)


def lanes_at(plane, start=0):
    return pl.ds(pl.multiple_of(start + plane * LANES, LANES), LANES)


def states_kernel(
    block_hbm, taps_hbm, small_hbm, end_ref, block_ref, taps_ref, small_ref, kb, vb, sems
):
    tokens, count = block_ref.shape[1:]
    poles = end_ref.shape[0]
    decay_ref = small_ref.at[0]
    steps = tokens // SUBLANES
    parts = sems.shape[0] - 3
    width = count // parts
    small = [
        pltpu.make_async_copy(source, target, sems.at[parts + i])
        for i, (source, target) in enumerate(
            [
                (taps_hbm, taps_ref),
                (small_hbm, small_ref),
                (block_hbm.at[:1], block_ref.at[:1]),
            ]
        )
    ]
    large = []
    for i in range(parts):
        lanes = pl.ds(i * width, width)
        large.append(
            pltpu.make_async_copy(
                block_hbm.at[1:, :, lanes], block_ref.at[1:, :, lanes], sems.at[i]
            )
        )
    for copy in large[:1] + small[:2] + large[1:] + small[2:]:
        copy.start()
    later = (SUBLANES - 1) - lax.broadcasted_iota(jnp.int32, (SUBLANES, LANES), 0)
    later = (later * steps + 1).astype(F32)

    def body(first, which, plane):
        lanes = lanes_at(plane, first)
        key = Convolved(block_ref, None, taps_ref, 1, lanes, kb.at[which])
        value = Convolved(block_ref, None, taps_ref, 2, lanes, vb.at[which])
        rates = [spread(decay_ref[r : r + 1, lanes]) for r in range(poles)]
        every = jnp.exp(-decay_ref[:, lanes])
        fades = [spread(every[r : r + 1]) for r in range(poles)]
        sums = None
        for j in range(steps):
            product = key(j) * value(j)
            if sums is None:
                sums = [product] * poles
            else:
                sums = [fades[r] * sums[r] + product for r in range(poles)]
        for r in range(poles):
            ended = sums[r] * jnp.exp(-rates[r] * later)
            end_ref[r : r + 1, lanes] = jnp.sum(ended, axis=0, keepdims=True)

    for copy in small[:2]:
        copy.wait()
    for i in range(parts):
        large[i].wait()
        over_planes(width, kb.shape[0], functools.partial(body, i * width))
    for copy in small[2:]:
        copy.wait()


def local_kernel(
    block_ref, halo_ref, taps_ref, small_ref, product_ref, query_ref, scan_ref, qb, kb, vb
):
    steps = product_ref.shape[1]
    poles = scan_ref.shape[1]
    place = lax.broadcasted_iota(jnp.int32, (SUBLANES, LANES), 0)

    def body(which, plane):
        lanes = lanes_at(plane)
        key = Convolved(block_ref, halo_ref, taps_ref, 1, lanes, kb.at[which])
        value = Convolved(block_ref, halo_ref, taps_ref, 2, lanes, vb.at[which])
        query = Convolved(block_ref, halo_ref, taps_ref, 0, lanes, qb.at[which])
        rates = small_ref[0, :, lanes]
        every = jnp.exp(-rates)
        fades = [spread(every[r : r + 1]) for r in range(poles)]
        sums = None
        for j in range(steps):
            product = key(j) * value(j)
            product_ref[plane, j] = product
            query_ref[plane, j] = query(j)
            if sums is None:
                sums = [product] * poles
            else:
                sums = [fades[r] * sums[r] + product for r in range(poles)]
        for r in range(poles):
            rate = spread(rates[r : r + 1])
            scan = fades[r] * sums[r]
            reach = 1
            while reach < SUBLANES:
                moved = jnp.where(place >= reach, pltpu.roll(scan, reach, 0), 0.0)
                scan = scan + jnp.exp(-rate * float(reach * steps)) * moved
                reach *= 2
            scan_ref[plane, r] = jnp.where(place >= 1, pltpu.roll(scan, 1, 0), 0.0)

    over_planes(block_ref.shape[2], kb.shape[0], body)


def gated_kernel(
    j, lines, place_ref, product_ref, query_ref, scan_ref, small_ref, prefix_ref, last_ref,
    *refs,
):
    *out_refs, ob = refs
    steps = product_ref.shape[1]
    tokens, share = steps * SUBLANES, out_refs[0].shape[1]
    poles = prefix_ref.shape[0]
    decay_ref, residues_ref, carried_ref = (small_ref.at[i] for i in range(3))
    half = lax.rem(place_ref[0] + j, lines)
    since_start = (place_ref[0] * tokens).astype(F32)
    since_last = (place_ref[1] * tokens).astype(F32)
    upper = place_ref[1] != place_ref[0]
    place = lax.broadcasted_iota(jnp.int32, (SUBLANES, LANES), 0)
    before = (place * steps).astype(F32)

    def body(which, plane):
        lanes = lanes_at(plane, half * share)
        held = half * (share // LANES) + plane
        rates = decay_ref[:, lanes]
        every = jnp.exp(-rates)
        state = jnp.exp(-rates * since_start) * carried_ref[:, lanes] + prefix_ref[:, lanes]
        last = jnp.exp(-rates * since_last) * last_ref[:, lanes]
        state = state + jnp.where(upper, last, 0.0)
        fades = [spread(every[r : r + 1]) for r in range(poles)]
        sums = []
        for r in range(poles):
            within = jnp.exp(-spread(rates[r : r + 1]) * before)
            sums.append(scan_ref[held, r] + within * spread(state[r : r + 1]))
        weights = [spread(residues_ref[r : r + 1, lanes]) for r in range(poles)]
        for j in range(steps):
            product = product_ref[held, j]
            if j:
                sums = [fades[r] * sums[r] + product for r in range(poles)]
            else:
                sums = [sums[r] + product for r in range(poles)]
            terms = [weights[r] * sums[r] for r in range(poles)]
            while len(terms) > 1:
                terms = [a + b for a, b in zip(terms[::2], terms[1::2])] + terms[len(terms) & ~1 :]
            ob[which, pl.ds(j, SUBLANES, stride=steps), :] = query_ref[held, j] * terms[0]
        for i, out_ref in enumerate(out_refs):
            rows = out_ref.shape[0]
            part = ob[which, i * rows : (i + 1) * rows]
            out_ref[:, lanes_at(plane)] = part.astype(out_ref.dtype)

    over_planes(share, ob.shape[0], body)


VMEM = pl.BlockSpec(memory_space=pltpu.VMEM)
SMEM = pl.BlockSpec(memory_space=pltpu.SMEM)
ROOM = pltpu.CompilerParams(vmem_limit_bytes=8 << 20)
TOGETHER = 2


def end_states(*arrays):
    features, _, small = arrays
    _, tokens, count = features.shape
    poles = small.shape[1]
    return pl.pallas_call(
        states_kernel,
        in_specs=[pl.BlockSpec(memory_space=pltpu.HBM)] * 3,
        out_specs=[VMEM] * 4,
        out_shape=[jax.ShapeDtypeStruct((poles, count), F32)]
        + [jax.ShapeDtypeStruct(array.shape, array.dtype) for array in arrays],
        scratch_shapes=[pltpu.VMEM((TOGETHER, PAD + tokens, LANES), F32)] * 2
        + [pltpu.SemaphoreType.DMA((math_gcd(count // LANES, 4) + 3,))],
        compiler_params=ROOM,
        cost_estimate=pl.CostEstimate(
            flops=4 * poles * tokens * count, bytes_accessed=6 * tokens * count, transcendentals=0
        ),
        name="end_states",
    )(*arrays)


def local_parts(features, halo, taps, small):
    _, tokens, count = features.shape
    poles = small.shape[1]
    rows = (count // LANES, tokens // SUBLANES, SUBLANES, LANES)
    scans = (count // LANES, poles, SUBLANES, LANES)
    return pl.pallas_call(
        local_kernel,
        in_specs=[VMEM] * 4,
        out_specs=[VMEM] * 3,
        out_shape=[jax.ShapeDtypeStruct(shape, F32) for shape in (rows, rows, scans)],
        scratch_shapes=[pltpu.VMEM((TOGETHER, PAD + tokens, LANES), F32)] * 3,
        compiler_params=ROOM,
        cost_estimate=pl.CostEstimate(
            flops=4 * poles * tokens * count, bytes_accessed=8 * tokens * count, transcendentals=0
        ),
        name="local_parts",
    )(features, halo, taps, small)


def gated_half(j, lines, parts, place, share, arrays, states):
    tokens = arrays[0].shape[1] * SUBLANES
    poles = states[0].shape[0]
    return pl.pallas_call(
        functools.partial(gated_kernel, j, lines),
        in_specs=[SMEM] + [VMEM] * (len(arrays) + len(states)),
        out_specs=[VMEM] * parts,
        out_shape=[jax.ShapeDtypeStruct((tokens // parts, share), BF16)] * parts,
        scratch_shapes=[pltpu.VMEM((TOGETHER, tokens, LANES), F32)],
        compiler_params=ROOM,
        cost_estimate=pl.CostEstimate(
            flops=4 * poles * tokens * share, bytes_accessed=8 * tokens * share, transcendentals=0
        ),
        name="gated_half",
    )(place, *arrays, *states)


def shards(stream_in, features, conv_taps, decay, residues, state_in, out_weight):
    seqs, chans = lax.axis_size("seq"), lax.axis_size("chan")
    both = ("seq", "chan")
    lines = seqs // chans
    bits = chans.bit_length() - 1
    tokens = features.shape[1]
    share, _ = out_weight.shape
    here = lax.axis_index("seq")
    turned = [sum(((c >> i) & 1) << (bits - 1 - i) for i in range(bits)) for c in range(chans)]
    places = [(a, b, c) for a in range(chans) for b in range(lines) for c in range(chans)]

    def number(a, b, c):
        return (a * lines + b) * chans + c

    def moved(block, target):
        return lax.ppermute(block, both, [(number(*p), number(*target(*p))) for p in places])

    reach = conv_taps.shape[1] - 1
    halo = lax.ppermute(
        features[:, tokens - reach :, :], "seq", [(s, s + 1) for s in range(seqs - 1)]
    )
    small = jnp.stack([decay.T, residues.T, state_in.T])
    ends, features, conv_taps, small = end_states(features, conv_taps, small)
    rates = small[0]
    parts = local_parts(features, halo, conv_taps, small)
    ends = ends + first_tokens(features[1:, :reach], halo[1:], conv_taps[1:], rates, tokens)
    prefix = jnp.zeros_like(ends)
    width = 1
    while True:
        other = lax.ppermute(ends, "seq", [(s, s ^ width) for s in range(seqs)])
        if 2 * width >= seqs:
            break
        upper = (here & width) != 0
        within = (here % width * tokens).astype(F32)
        fade = jnp.exp(-rates * float(width * tokens))
        prefix = prefix + jnp.where(upper, jnp.exp(-rates * within) * other, 0.0)
        ends = jnp.where(upper, ends + fade * other, other + fade * ends)
        width *= 2

    order = list(range(1, lines)) + [0]
    place = jnp.stack([here, here % width]).astype(jnp.int32)
    top = chans >> 1
    blocks = {}
    for j in order:
        results = gated_half(
            j, lines, 2 if j else 1, place, share, (*parts, small), (prefix, other),
        )
        blocks[j] = [moved(results[0], lambda a, b, c: (c, (b + j) % lines, turned[a ^ c]))]
        if j:
            other_half = moved(results[1], lambda a, b, c: (a, b, c ^ top))
            blocks[j].append(
                moved(other_half, lambda a, b, c: (c ^ top, (b + j) % lines, turned[a ^ c ^ top]))
            )

    odd = lax.axis_index("chan") % 2 == 1
    pieces = {}
    for j in order:
        lower, sides = [], []
        for p, block in enumerate(blocks[j]):
            lower.append(block)
            sides.append(moved(block, lambda a, b, c: (a, b, c ^ 1)))
            if j:
                pieces[j, 0, 0, p] = product_of(jnp.where(odd, lower[p], sides[p]), out_weight, j)
        if len(lower) > 1:
            lower, sides = [jnp.concatenate(lower, axis=0)], [jnp.concatenate(sides, axis=0)]
        for i in range(bits - 1):
            flip = top >> i
            for slot in range(1 << i):
                new = slot + (1 << i)
                lower.append(moved(lower[slot], lambda a, b, c: (a, b, c ^ flip)))
                sides.append(moved(lower[new], lambda a, b, c: (a, b, c ^ 1)))
        for slot in range(top):
            for group, pair in enumerate([(lower[slot], sides[slot]), (sides[slot], lower[slot])]):
                if (j, group, slot, 0) not in pieces:
                    pieces[j, group, slot, 0] = product_of(jnp.where(odd, *pair), out_weight, j)

    half = tokens // 2
    total = stream_in.astype(F32)
    for group in range(2):
        for slot in range(top):
            cut = group == 1 or slot == 0
            own = [pieces[0, group, slot, 0]]
            if cut:
                own = lax.optimization_barrier((own[0][:half], own[0][half:]))
            came = []
            for p, mixed in enumerate(own):
                for j in range(1, lines):
                    if group:
                        part = pieces[j, group, slot, 0][p * half : (p + 1) * half]
                    else:
                        part = pieces[j, group, slot, p]
                    part = moved(part, lambda a, b, c: (a, (b - j) % lines, c))
                    mixed = mixed + part.astype(F32)
                    mixed = mixed.astype(BF16) if j == lines - 1 else mixed

                def target(a, b, c):
                    return a ^ turned[c] ^ (slot + top * (c % 2 == group)), b, c

                came.append(moved(mixed, target))
            total = total + (jnp.concatenate(came, axis=0) if cut else came[0]).astype(F32)
    return total.astype(BF16)


def product_of(block, weight, j):
    product = jnp.dot(block, weight, preferred_element_type=F32)
    return product.astype(BF16) if j else lax.optimization_barrier(product)


def first_tokens(features, halo, taps, rates, tokens):
    features, halo = features.astype(F32), halo.astype(F32)
    reach = halo.shape[1]
    total = jnp.zeros_like(rates)
    for t in range(reach):
        inner = sum(taps[:, k] * features[:, t - k] for k in range(t + 1))
        outer = sum(taps[:, k] * halo[:, reach + t - k] for k in range(t + 1, reach + 1))
        change = inner[0] * outer[1] + outer[0] * (inner[1] + outer[1])
        total = total + jnp.exp(-rates * float(tokens - t)) * change
    return total


def solution(mesh):
    return jax.shard_map(
        shards,
        mesh=mesh,
        in_specs=(
            P("seq", "chan"),
            P(None, "seq", "chan"),
            P(None, None, "chan"),
            P("chan", None),
            P("chan", None),
            P("chan", None),
            P("seq", "chan"),
        ),
        out_specs=P("seq", "chan"),
        check_vma=False,
    )
```
